32 devices in a mesh: dp: 2 (over x), ctx: 4 (over y, core), tensor: 4 (over z).
Axes of the slice: x: 2, y: 2, z: 4, core: 2. Of those that a mesh axis runs over, the one named last changes fastest.
Arguments:
- hidden: bfloat16 [2, 8, 1024, 768], P(None, ('dp', 'tensor'), 'ctx'), may hold values from -6 to 6
- segment_ids: int32 [2, 8, 1024], P(None, ('dp', 'tensor')), may hold values from 0 to 3, never falling along the last dimension, each value on 1 to 512 neighbouring positions
- w_in: bfloat16 [768, 1536], P('dp'), may hold values from -0.21875 to 0.21875
- w_depth: bfloat16 [768, 9], P('dp'), may hold values from -2 to 2
- w_point: bfloat16 [768, 384], P('dp'), may hold values from -0.21875 to 0.21875
- w_kernel: bfloat16 [384, 54], P('dp'), may hold values from -0.3125 to 0.3125
- w_out: bfloat16 [768, 768], P('dp'), may hold values from -2 to 2
- norm1_gain: bfloat16 [768], P('dp'), may hold values from 0.5 to 1.5
- norm1_bias: bfloat16 [768], P('dp'), may hold values from -3 to 3
- norm2_gain: bfloat16 [768], P('dp'), may hold values from 0.5 to 1.5
- norm2_bias: bfloat16 [768], P('dp'), may hold values from -3 to 3
- w_up: bfloat16 [384, 2, 1536], P('dp', None, 'tensor'), may hold values from -0.3125 to 0.3125
- w_down: bfloat16 [384, 2, 1536], P('dp', None, 'tensor'), may hold values from -0.15625 to 0.15625
- out_grad: bfloat16 [2, 8, 1024, 768], P(None, ('dp', 'tensor'), 'ctx'), may hold values from -6 to 6
Outputs:
- output: bfloat16 [2, 8, 1024, 768], P(None, ('dp', 'tensor'), 'ctx')
- input_grad: bfloat16 [2, 8, 1024, 768], P(None, ('dp', 'tensor'), 'ctx')
- w_in_grad: float32 [768, 1536], P('dp')
- w_depth_grad: float32 [768, 9], P('dp')
- w_point_grad: float32 [768, 384], P('dp')
- w_kernel_grad: float32 [384, 54], P('dp')
- w_out_grad: float32 [768, 768], P('dp')
- norm1_gain_grad: float32 [768], P('dp')
- norm1_bias_grad: float32 [768], P('dp')
- norm2_gain_grad: float32 [768], P('dp')
- norm2_bias_grad: float32 [768], P('dp')
- w_up_grad: float32 [384, 2, 1536], P('dp', None, 'tensor')
- w_down_grad: float32 [384, 2, 1536], P('dp', None, 'tensor')
The draws below stay inside these ranges and needn't reach their ends.
Inputs may be any that keep to these rules, and one draw needn't show every extreme that they name: `segment_ids`: along each sequence the numbers never fall; every document has 1 to 512 positions, and one has exactly 512.
All inputs are finite; a program needn't handle non-finite values.
Results may differ from the reference program's by a relative error of at most 0.017.
Values may be sent and summed in bfloat16 or wider, within the bound.
No kernel may reach another device: no remote copies, remote signals or barrier semaphores. Data moves between devices by JAX's collectives and lax.ppermute only.
A program may use at most 256 MiB of HBM per device.

```python
import math
import jax
import jax.numpy as jnp
import numpy as np
from jax import lax

D = 768
HEADS = 6
HEAD_DIM = 64
KERNEL = 9
FF = 3072
GROUPS = 2
MICRO = 2
SEQS = 8
SEQ_LEN = 1024
DOCS = 4
DOC_MOST = 512


def draw_w_out(key, part):
    normal_draw = jnp.clip(jax.random.normal(key, (D, D), jnp.float32), -5.0, 5.0)
    row_index = jnp.arange(D)[:, None]
    return (jnp.where(row_index < HEADS * HEAD_DIM, 0.4, 0.09) * normal_draw).astype(jnp.bfloat16)


def steps_of(key, shape, cuts, low, high):
    gain, own = 1.0, jax.random.fold_in(key, 6)
    for dim, shards_of in cuts:
        heights = jnp.exp(jax.random.uniform(jax.random.fold_in(own, dim), (shards_of,), jnp.float32, low / len(cuts), high / len(cuts)))
        gain = gain * jnp.repeat(heights, shape[dim] // shards_of).reshape([-1 if axis == dim else 1 for axis in range(len(shape))])
    return gain


def length_profile(amount, total, limit, lean):
    portions = [(1 << 20) // math.isqrt(grade ** lean) + 1 for grade in range(2, amount + 1)]
    surplus, holding = total - limit - (amount - 1), [1] * (amount - 1)
    while surplus > 0:
        candidates = [i for i in range(amount - 1) if holding[i] < limit]
        pool, budget = sum([portions[i] for i in candidates]), surplus
        for i in candidates:
            extra = min(limit - holding[i], max(1, budget * portions[i] // pool), surplus)
            holding[i] = holding[i] + extra
            surplus = surplus - extra
    return np.array([limit] + holding)


def ragged_sizes(rng, amount, total, reach, skew):
    if amount == 2:
        one = jax.random.randint(rng, (), max(1, total - reach), min(reach, total - 1) + 1)
        return jnp.stack([one, total - one])
    tallies = jnp.asarray(length_profile(amount, total, reach, skew), jnp.int32)
    couples = (amount - 1) // 2
    source_of, sink = tallies[1:1 + 2 * couples:2], tallies[2:2 + 2 * couples:2]
    slack = jnp.minimum(source_of - 1, reach - sink)
    passed = jax.random.randint(jax.random.fold_in(rng, 1), (couples,), 0, 1 << 20) % (slack + 1)
    tallies = tallies.at[1:1 + 2 * couples:2].set(source_of - passed).at[2:2 + 2 * couples:2].set(sink + passed)
    return tallies[jax.random.permutation(jax.random.fold_in(rng, 2), amount)]


def noise(rng, dims, scale, limit, shards=(), kind=jnp.bfloat16):
    loudness = steps_of(rng, dims, shards, -0.22, 0.18) if shards else 1.0
    entries = jax.random.normal(rng, dims, jnp.float32) * scale * loudness
    return jnp.minimum(jnp.maximum(entries, -limit), limit).astype(kind)


def setup_inputs(seed: int = 0) -> dict:
    key_of = jax.random.split(jax.random.key(seed), 15)
    hidden = noise(key_of[0], (MICRO, SEQS, SEQ_LEN, D), 1.0, 6.0, ((1, 8), (2, 4)))
    segment_ids = jax.vmap(lambda own: jnp.searchsorted(jnp.cumsum(ragged_sizes(own, DOCS, SEQ_LEN, DOC_MOST, 1)), jnp.arange(SEQ_LEN), side="right"))(jax.random.split(key_of[1], MICRO * SEQS)).reshape((MICRO, SEQS, SEQ_LEN)).astype(jnp.int32)
    w_in = noise(key_of[2], (D, 4 * HEADS * HEAD_DIM), D ** -0.5, 0.21875, ((0, 2),))
    w_depth = noise(key_of[3], (D, KERNEL), KERNEL ** -0.5, 2.0, ((0, 2),))
    w_point = noise(key_of[4], (D, HEADS * HEAD_DIM), D ** -0.5, 0.21875, ((0, 2),))
    w_kernel = noise(key_of[5], (HEADS * HEAD_DIM, HEADS * KERNEL), (HEADS * HEAD_DIM) ** -0.5, 0.3125, ((0, 2),))
    w_out = draw_w_out(jax.random.fold_in(key_of[14], 71), 0)
    norm1_gain = jnp.clip(1.0 + 0.1 * jax.random.normal(key_of[7], (D,), jnp.float32), 0.5, 1.5).astype(jnp.bfloat16)
    norm1_bias = noise(key_of[8], (D,), 0.3, 3.0, ((0, 2),))
    norm2_gain = jnp.clip(1.0 + 0.1 * jax.random.normal(key_of[9], (D,), jnp.float32), 0.5, 1.5).astype(jnp.bfloat16)
    norm2_bias = noise(key_of[10], (D,), 0.3, 3.0, ((0, 2),))
    w_up = noise(key_of[11], (D // GROUPS, GROUPS, FF // GROUPS), (D // GROUPS) ** -0.5, 0.3125, ((0, 2), (2, 4)))
    w_down = noise(key_of[12], (D // GROUPS, GROUPS, FF // GROUPS), (FF // GROUPS) ** -0.5, 0.15625, ((0, 2), (2, 4)))
    out_grad = noise(key_of[13], (MICRO, SEQS, SEQ_LEN, D), 1.0, 6.0, ((1, 8), (2, 4)))
    return {"hidden": hidden, "segment_ids": segment_ids, "w_in": w_in, "w_depth": w_depth, "w_point": w_point, "w_kernel": w_kernel, "w_out": w_out, "norm1_gain": norm1_gain, "norm1_bias": norm1_bias, "norm2_gain": norm2_gain, "norm2_bias": norm2_bias, "w_up": w_up, "w_down": w_down, "out_grad": out_grad}


NORM_EPS = 1e-05
NEG_FILL = -1e+30
HIGHEST = lax.Precision.HIGHEST

@jax.custom_vjp
def low(v):
    return lax.optimization_barrier(v.astype(jnp.bfloat16)).astype(jnp.float32)

@jax.custom_vjp
def low_back(v):
    return v

def low_keep(v):
    return (low(v), None)

def low_pass(kept, grad):
    return (grad,)

def back_keep(v):
    return (v, None)

def back_low(kept, grad):
    return (low(grad),)
low.defvjp(low_keep, low_pass)
low_back.defvjp(back_keep, back_low)

def matmul(left, right):
    return jnp.dot(left, right, precision=HIGHEST)

def gelu_exact(values):
    return 0.5 * values * (1.0 + jax.scipy.special.erf(values * 0.7071067811865476))

def softmax_last(values):
    shifted = values - lax.optimization_barrier(jnp.max(values, axis=-1, keepdims=True))
    expo_vals = jnp.exp(shifted)
    return expo_vals / lax.optimization_barrier(jnp.sum(expo_vals, axis=-1, keepdims=True))

def layer_norm(values, gain_vec, bias_vec):
    average = lax.optimization_barrier(jnp.mean(values, axis=-1, keepdims=True))
    centred = values - average
    variance = lax.optimization_barrier(jnp.mean(centred * centred, axis=-1, keepdims=True))
    return centred * lax.rsqrt(variance + NORM_EPS) * gain_vec + bias_vec

def sequence(tokens, seq_ids, params):
    w_in, w_depth, w_point, w_kernel, w_out, gain_one, bias_one, gain_two, bias_two, w_up, w_down = params
    length = tokens.shape[0]
    attn_width = HEADS * HEAD_DIM
    radius = KERNEL // 2
    projected = low_back(low(matmul(tokens, w_in)))
    queries = projected[:, :attn_width]
    key_rows = projected[:, attn_width:2 * attn_width]
    value_rows = projected[:, 2 * attn_width:3 * attn_width]
    conv_rows = projected[:, 3 * attn_width:]
    padded_ids = jnp.pad(seq_ids, radius, constant_values=-1)
    tap_mask = jnp.stack([padded_ids[j:j + length] == seq_ids for j in range(KERNEL)], axis=1).astype(jnp.float32)
    pad_tokens = jnp.pad(tokens, ((radius, radius), (0, 0)))
    pre_key = sum((pad_tokens[j:j + length] * w_depth[:, j] * tap_mask[:, j:j + 1] for j in range(KERNEL)))
    conv_key = low_back(matmul(low(pre_key), w_point))
    mixed = low_back(low(conv_key * queries))
    logits = matmul(mixed, w_kernel).reshape(length, HEADS, KERNEL)
    kernels = softmax_last(logits)
    pad_conv = jnp.pad(conv_rows, ((radius, radius), (0, 0))).reshape(length + 2 * radius, HEADS, HEAD_DIM)
    conv_out = sum((kernels[:, :, j:j + 1] * tap_mask[:, j, None, None] * pad_conv[j:j + length] for j in range(KERNEL)))
    heads_q = queries.reshape(length, HEADS, HEAD_DIM)
    heads_k = key_rows.reshape(length, HEADS, HEAD_DIM)
    heads_v = value_rows.reshape(length, HEADS, HEAD_DIM)
    raw_scores = jnp.einsum('qhd,khd->hqk', heads_q, heads_k, precision=HIGHEST) * HEAD_DIM ** (-0.5)
    scores = low_back(raw_scores)
    same_doc = (seq_ids[:, None] == seq_ids[None, :])[None]
    attn_probs = softmax_last(jnp.where(same_doc, scores, NEG_FILL))
    attn_out = jnp.einsum('hqk,khd->qhd', low(attn_probs), heads_v, precision=HIGHEST)
    context = low_back(low(jnp.concatenate([attn_out.reshape(length, attn_width), conv_out.reshape(length, attn_width)], axis=1)))
    mixed_out = low_back(matmul(context, w_out))
    normed_one = layer_norm(tokens + mixed_out, gain_one, bias_one)
    rows_grouped = low(normed_one).reshape(length, GROUPS, D // GROUPS)
    up_proj = low_back(jnp.einsum('rgi,igj->rgj', rows_grouped, w_up, precision=HIGHEST))
    activated = low(gelu_exact(up_proj))
    down_proj = low_back(jnp.einsum('rgj,igj->rgi', activated, w_down, precision=HIGHEST).reshape(length, D))
    return layer_norm(normed_one + down_proj, gain_two, bias_two)

def reference(hidden, segment_ids, w_in, w_depth, w_point, w_kernel, w_out, norm1_gain, norm1_bias, norm2_gain, norm2_bias, w_up, w_down, out_grad):
    params = tuple((weight_arr.astype(jnp.float32) for weight_arr in (w_in, w_depth, w_point, w_kernel, w_out, norm1_gain, norm1_bias, norm2_gain, norm2_bias, w_up, w_down)))
    seq_count = MICRO * SEQS
    all_tokens = hidden.astype(jnp.float32).reshape(seq_count, SEQ_LEN, D)
    all_ids = segment_ids.reshape(seq_count, SEQ_LEN).astype(jnp.int32)

    def forward(token_arr, weight_set):

        def single_sequence(inputs_pair):
            return sequence(inputs_pair[0], inputs_pair[1], weight_set)
        return lax.map(jax.checkpoint(single_sequence), (token_arr, all_ids))
    outputs, pullback = jax.vjp(forward, all_tokens, params)
    grad_tokens, grad_params = pullback(out_grad.astype(jnp.float32).reshape(seq_count, SEQ_LEN, D))
    full_shape = hidden.shape
    return (outputs.astype(jnp.bfloat16).reshape(full_shape), grad_tokens.astype(jnp.bfloat16).reshape(full_shape), grad_params[0], grad_params[1], grad_params[2], grad_params[3], grad_params[4], grad_params[5], grad_params[6], grad_params[7], grad_params[8], grad_params[9], grad_params[10])
```

```python
import math

import jax
import jax.numpy as jnp
from jax import lax
from jax.sharding import PartitionSpec as P

D = 768
HEADS = 6
HEAD_DIM = 64
KERNEL = 9
GROUPS = 2
MICRO = 2


NORM_EPS = 1e-05
NEG_FILL = -1e30
HIGHEST = lax.Precision.HIGHEST


def padded(block, sides, width):
    for axis, dim in sides:
        count = lax.axis_size(axis)
        forward = [(i, i + 1) for i in range(count - 1)]
        backward = [(target, source) for source, target in forward]
        low = lax.ppermute(
            lax.slice_in_dim(block, block.shape[dim] - width, None, axis=dim), axis, forward
        )
        high = lax.ppermute(lax.slice_in_dim(block, 0, width, axis=dim), axis, backward)
        block = jnp.concatenate([low, block, high], axis=dim)
    return block


def swap(block, axis, bit):
    count = lax.axis_size(axis)
    return lax.ppermute(block, axis, [(i, i ^ bit) for i in range(count)])


def bit_set(axis, bit):
    return (lax.axis_index(axis) // bit) % 2 == 1


def pick(pair, take_high):
    return jnp.where(take_high, pair[1], pair[0])


def halves(block, dim):
    size = block.shape[dim] // 2
    return (
        lax.slice_in_dim(block, 0, size, axis=dim),
        lax.slice_in_dim(block, size, 2 * size, axis=dim),
    )


def fold(block, axis, bit, dim):
    high = bit_set(axis, bit)
    low_half, high_half = halves(block, dim)
    sent = jnp.where(high, low_half, high_half)
    kept = jnp.where(high, high_half, low_half)
    arrived = swap(sent, axis, bit)
    return (kept.astype(jnp.float32) + arrived.astype(jnp.float32)).astype(block.dtype)


def unfold(block, axis, bit, dim):
    other = swap(block, axis, bit)
    high = bit_set(axis, bit)
    return jnp.concatenate(
        [jnp.where(high, other, block), jnp.where(high, block, other)], axis=dim
    )


def bits_of(axis):
    bits, bit = [], 1
    while bit < lax.axis_size(axis):
        bits.append(bit)
        bit *= 2
    return bits


def gather_rows(block, axis):
    depth = 0
    shape = block.shape
    for bit in reversed(bits_of(axis)):
        other = swap(block, axis, bit)
        high = bit_set(axis, bit)
        block = jnp.stack([jnp.where(high, other, block), jnp.where(high, block, other)], axis=depth)
        depth += 1
    return block.reshape((-1,) + shape[1:])


def scatter_rows(block, axis):
    bits = bits_of(axis)
    block = block.reshape((2,) * len(bits) + (-1,) + block.shape[1:])
    for bit in bits:
        dim = len([b for b in bits if b > bit])
        block = fold(block, axis, bit, dim)
        block = lax.squeeze(block, (dim,))
    return block


def line_gather(block, axis):
    count = lax.axis_size(axis)
    up = [(i, i + 1) for i in range(count - 1)]
    down = [(i + 1, i) for i in range(count - 1)]
    lower, upper = [], []
    from_low, from_high = block, block
    for _ in range(count - 1):
        from_low = lax.ppermute(from_low, axis, up)
        from_high = lax.ppermute(from_high, axis, down)
        lower.insert(0, from_low)
        upper.append(from_high)
    line = jnp.stack(lower + [block] + upper)
    return lax.dynamic_slice_in_dim(line, count - 1 - lax.axis_index(axis), count, axis=0)


def pair_share(block, dim):
    high = bit_set("ctx", 1)
    part = pick(halves(block, dim), high)
    arrived = swap(part, "dp", 1)
    other = unfold(arrived, "ctx", 1, dim)
    on_high = bit_set("dp", 1)
    return jnp.concatenate([jnp.where(on_high, other, block), jnp.where(on_high, block, other)], axis=0)


def fit(block, rows, columns):
    return jnp.pad(block, ((0, rows - block.shape[0]), (0, columns - block.shape[1])))


def gelu_exact(values):
    return 0.5 * values * (1.0 + jax.scipy.special.erf(values * 0.7071067811865476))


def softmax_last(values):
    shifted = values - jnp.max(values, axis=-1, keepdims=True)
    expo_vals = jnp.exp(shifted)
    return expo_vals / jnp.sum(expo_vals, axis=-1, keepdims=True)


def rows_product(left, right):
    return lax.dot_general(
        left, right, (((0,), (0,)), ((), ())), preferred_element_type=jnp.float32
    )


def times_transposed(left, right):
    return lax.dot_general(
        left, right, (((1,), (1,)), ((), ())), preferred_element_type=jnp.float32
    )


def norm_forward(values, gain_vec, bias_vec):
    average = jnp.mean(values, axis=-1, keepdims=True)
    centred = values - average
    inverse = lax.rsqrt(jnp.mean(centred * centred, axis=-1, keepdims=True) + NORM_EPS)
    normalized = centred * inverse
    return (normalized * gain_vec + bias_vec, normalized, inverse)


def norm_backward(grad_out, normalized, inverse, gain_vec):
    scaled = grad_out * gain_vec
    inner = (
        scaled
        - jnp.mean(scaled, axis=-1, keepdims=True)
        - normalized * jnp.mean(scaled * normalized, axis=-1, keepdims=True)
    )
    return (inner * inverse, jnp.sum(grad_out * normalized, axis=0), jnp.sum(grad_out, axis=0))


def meets(query_ids, key_ids):
    return jnp.logical_and(key_ids[0] <= query_ids[-1], key_ids[-1] >= query_ids[0])


def block_scores(heads_q, key_block, query_ids, key_ids, score_scale):
    raw_scores = (
        jnp.einsum("qhd,khd->hqk", heads_q, key_block, preferred_element_type=jnp.float32)
        * score_scale
    )
    return jnp.where((query_ids[:, None] == key_ids[None, :])[None], raw_scores, NEG_FILL)


def keep_state(state):
    return state


def log_totals(heads_q, key_blocks, query_ids, id_blocks, score_scale):
    head_count = heads_q.shape[1]
    row_count = heads_q.shape[0]

    def log_scan_step(carried, inputs):

        def log_visit(state):
            running, summed = state
            scores = block_scores(heads_q, inputs[0], query_ids, inputs[1], score_scale)
            highest = jnp.maximum(running, jnp.max(scores, axis=-1))
            summed = summed * jnp.exp(running - highest) + jnp.sum(
                jnp.exp(scores - highest[..., None]), axis=-1
            )
            return (highest, summed)

        return (lax.cond(meets(query_ids, inputs[1]), log_visit, keep_state, carried), None)

    start_state = (
        jnp.full((head_count, row_count), NEG_FILL, jnp.float32),
        jnp.zeros((head_count, row_count), jnp.float32),
    )
    final_state, unused = lax.scan(log_scan_step, start_state, (key_blocks, id_blocks))
    return final_state[0] + jnp.log(final_state[1])


def attend(heads_q, key_blocks, value_blocks, query_ids, id_blocks, log_total, score_scale):

    def attend_scan_step(carried, inputs):

        def attend_visit(state):
            scores = block_scores(heads_q, inputs[0], query_ids, inputs[2], score_scale)
            weights = jnp.exp(scores - log_total[..., None]).astype(jnp.bfloat16)
            return state + jnp.einsum(
                "hqk,khd->qhd", weights, inputs[1], preferred_element_type=jnp.float32
            )

        return (lax.cond(meets(query_ids, inputs[2]), attend_visit, keep_state, carried), None)

    result, unused = lax.scan(
        attend_scan_step,
        jnp.zeros(heads_q.shape, jnp.float32),
        (key_blocks, value_blocks, id_blocks),
    )
    return result


def delta_pass(
    heads_q, grad_heads, key_blocks, value_blocks, query_ids, id_blocks, log_total, score_scale
):

    def delta_scan_step(carried, inputs):

        def delta_visit(state):
            scores = block_scores(heads_q, inputs[0], query_ids, inputs[2], score_scale)
            attn_probs = jnp.exp(scores - log_total[..., None])
            grad_probs = jnp.einsum(
                "qhd,khd->hqk", grad_heads, inputs[1], preferred_element_type=jnp.float32
            )
            return state + jnp.sum(attn_probs * grad_probs, axis=-1)

        return (lax.cond(meets(query_ids, inputs[2]), delta_visit, keep_state, carried), None)

    result, unused = lax.scan(
        delta_scan_step,
        jnp.zeros(log_total.shape, jnp.float32),
        (key_blocks, value_blocks, id_blocks),
    )
    return result


def score_grads(
    heads_q, grad_heads, key_block, value_block, query_ids, key_ids, log_total, delta, score_scale
):
    scores = block_scores(heads_q, key_block, query_ids, key_ids, score_scale)
    attn_probs = jnp.exp(scores - log_total[..., None])
    grad_probs = jnp.einsum(
        "qhd,khd->hqk", grad_heads, value_block, preferred_element_type=jnp.float32
    )
    grad_scores = (attn_probs * (grad_probs - delta[..., None])).astype(jnp.bfloat16)
    return (grad_scores, attn_probs.astype(jnp.bfloat16))


def full_grad_pass(
    heads_q,
    grad_heads,
    key_blocks,
    value_blocks,
    query_ids,
    id_blocks,
    log_total,
    delta,
    score_scale,
):

    def full_scan_step(carried, inputs):
        key_block, value_block, key_ids = inputs
        block_len = key_block.shape[0]
        pair_width = 2 * key_block.shape[1] * key_block.shape[2]

        def full_visit(grad_query):
            grad_scores, probs_low = score_grads(
                heads_q,
                grad_heads,
                key_block,
                value_block,
                query_ids,
                key_ids,
                log_total,
                delta,
                score_scale,
            )
            grad_query = (
                grad_query
                + jnp.einsum(
                    "hqk,khd->qhd", grad_scores, key_block, preferred_element_type=jnp.float32
                )
                * score_scale
            )
            key_grad = (
                jnp.einsum("hqk,qhd->khd", grad_scores, heads_q, preferred_element_type=jnp.float32)
                * score_scale
            )
            value_grad = jnp.einsum(
                "hqk,qhd->khd", probs_low, grad_heads, preferred_element_type=jnp.float32
            )
            return (
                grad_query,
                jnp.concatenate(
                    [key_grad.reshape(block_len, -1), value_grad.reshape(block_len, -1)], axis=1
                ),
            )

        def skip_block(grad_query):
            return (grad_query, jnp.zeros((block_len, pair_width), jnp.float32))

        return lax.cond(meets(query_ids, key_ids), full_visit, skip_block, carried)

    grad_query, stacked = lax.scan(
        full_scan_step, jnp.zeros(heads_q.shape, jnp.float32), (key_blocks, value_blocks, id_blocks)
    )
    return (grad_query, stacked.reshape(-1, stacked.shape[-1]))


def body(
    hidden,
    segment_ids,
    w_in,
    w_depth,
    w_point,
    w_kernel,
    w_out,
    norm1_gain,
    norm1_bias,
    norm2_gain,
    norm2_bias,
    w_up,
    w_down,
    out_grad,
):
    on_high_core = bit_set("ctx", 1)
    full_in = pair_share(w_in, 0)
    half_rows = w_in.shape[0]
    kernel_rows = w_kernel.shape[0]
    vectors = jnp.stack([norm1_gain, norm1_bias, norm2_gain, norm2_bias], axis=1)
    small = fit(
        jnp.concatenate([w_depth, vectors, fit(w_kernel, half_rows, HEADS * KERNEL)], axis=1),
        half_rows,
        128,
    )
    packed = pair_share(jnp.concatenate([w_out, w_point, small], axis=1), 0)
    full_out = packed[:, :D]
    full_point = packed[:, D : D + HEADS * HEAD_DIM]
    small = packed[:, D + HEADS * HEAD_DIM :]
    full_depth = small[:, :KERNEL]
    gain_one, bias_one, gain_two, bias_two = (small[:, KERNEL + i] for i in range(4))
    full_kernel = small[:, KERNEL + 4 : KERNEL + 4 + HEADS * KERNEL]
    full_kernel = jnp.concatenate(
        [full_kernel[:kernel_rows], full_kernel[half_rows : half_rows + kernel_rows]], axis=0
    )
    line = line_gather(jnp.where(on_high_core, w_down, w_up), "tensor")
    both = unfold(line, "dp", 1, 1)
    both = jnp.transpose(both, (1, 2, 0, 3)).reshape(2 * w_up.shape[0], GROUPS, -1)
    other_both = swap(both, "ctx", 1)
    full_up = jnp.where(on_high_core, other_both, both)
    full_down = jnp.where(on_high_core, both, other_both)
    piece_rows = hidden.shape[2]
    seq_len = segment_ids.shape[2]
    attn_width = HEADS * HEAD_DIM
    radius = KERNEL // 2
    group_width = D // GROUPS
    block_rows = math.gcd(seq_len, 1024)
    block_count = seq_len // block_rows
    score_scale = HEAD_DIM ** (-0.5)
    row_offset = lax.axis_index("ctx") * piece_rows
    depth_table = full_depth.astype(jnp.float32)
    kernel_table = full_kernel.astype(jnp.float32)
    gain_one_f = gain_one.astype(jnp.float32)
    bias_one_f = bias_one.astype(jnp.float32)
    gain_two_f = gain_two.astype(jnp.float32)
    bias_two_f = bias_two.astype(jnp.float32)
    grad_totals = [
        jnp.zeros(weight_arr.shape, jnp.float32)
        for weight_arr in (
            full_in,
            full_depth,
            full_point,
            full_kernel,
            full_out,
            gain_one,
            bias_one,
            gain_two,
            bias_two,
            full_up,
            full_down,
        )
    ]
    outputs_list = []
    input_grads = []
    for micro_index in range(MICRO):
        tokens = hidden[micro_index, 0]
        cotangent = out_grad[micro_index, 0].astype(jnp.float32)
        seq_ids = segment_ids[micro_index, 0]
        own_ids = lax.dynamic_slice_in_dim(seq_ids, row_offset, piece_rows)
        window_ids = lax.dynamic_slice_in_dim(
            jnp.pad(seq_ids, radius, constant_values=-1), row_offset, piece_rows + 2 * radius
        )
        tap_mask = jnp.stack(
            [window_ids[j : j + piece_rows] == own_ids for j in range(KERNEL)], axis=1
        ).astype(jnp.float32)
        projected = jnp.dot(tokens, full_in, preferred_element_type=jnp.float32).astype(
            jnp.bfloat16
        )
        queries = projected[:, :attn_width]
        key_rows = projected[:, attn_width : 2 * attn_width]
        value_rows = projected[:, 2 * attn_width : 3 * attn_width]
        conv_rows = projected[:, 3 * attn_width :]
        extended = padded(jnp.concatenate([tokens, conv_rows], axis=1), (("ctx", 0),), radius)
        ext_tokens = extended[:, :D].astype(jnp.float32)
        ext_conv = (
            extended[:, D:].astype(jnp.float32).reshape(piece_rows + 2 * radius, HEADS, HEAD_DIM)
        )
        pre_key = sum(
            (
                ext_tokens[j : j + piece_rows] * depth_table[:, j] * tap_mask[:, j : j + 1]
                for j in range(KERNEL)
            )
        )
        pre_key_low = pre_key.astype(jnp.bfloat16)
        conv_key = jnp.dot(pre_key_low, full_point, preferred_element_type=jnp.float32)
        query_f = queries.astype(jnp.float32)
        mixed_low = (conv_key * query_f).astype(jnp.bfloat16)
        logits = jnp.dot(mixed_low, full_kernel, preferred_element_type=jnp.float32).reshape(
            piece_rows, HEADS, KERNEL
        )
        kernels = softmax_last(logits)
        conv_out = sum(
            (
                kernels[:, :, j : j + 1] * tap_mask[:, j, None, None] * ext_conv[j : j + piece_rows]
                for j in range(KERNEL)
            )
        )
        whole_kv = gather_rows(projected[:, attn_width : 3 * attn_width], "ctx")
        whole_keys, whole_values = whole_kv[:, :attn_width], whole_kv[:, attn_width:]
        heads_q = queries.reshape(piece_rows, HEADS, HEAD_DIM)
        key_blocks = whole_keys.reshape(block_count, block_rows, HEADS, HEAD_DIM)
        value_blocks = whole_values.reshape(block_count, block_rows, HEADS, HEAD_DIM)
        id_blocks = seq_ids.reshape(block_count, block_rows)
        log_total = log_totals(heads_q, key_blocks, own_ids, id_blocks, score_scale)
        attn_out = attend(
            heads_q, key_blocks, value_blocks, own_ids, id_blocks, log_total, score_scale
        )
        context = jnp.concatenate(
            [attn_out.reshape(piece_rows, attn_width), conv_out.reshape(piece_rows, attn_width)],
            axis=1,
        ).astype(jnp.bfloat16)
        mixed_out = jnp.dot(context, full_out, preferred_element_type=jnp.float32)
        normed_one, normal_one, inverse_one = norm_forward(
            tokens.astype(jnp.float32) + mixed_out, gain_one_f, bias_one_f
        )
        ffn_in = normed_one.astype(jnp.bfloat16)
        rows_grouped = ffn_in.reshape(-1, GROUPS, group_width)
        up_proj = jnp.einsum(
            "rgi,igj->rgj", rows_grouped, full_up, preferred_element_type=jnp.float32
        )
        activated = gelu_exact(up_proj).astype(jnp.bfloat16)
        down_proj = jnp.einsum(
            "rgj,igj->rgi", activated, full_down, preferred_element_type=jnp.float32
        ).reshape(piece_rows, D)
        final_rows, normal_two, inverse_two = norm_forward(
            normed_one + down_proj, gain_two_f, bias_two_f
        )
        outputs_list.append(final_rows.astype(jnp.bfloat16))
        grad_z, gain_two_grad, bias_two_grad = norm_backward(
            cotangent, normal_two, inverse_two, gain_two_f
        )
        grad_down = grad_z.astype(jnp.bfloat16)
        grad_grouped = grad_down.reshape(-1, GROUPS, group_width)
        grad_act = jnp.einsum(
            "rgi,igj->rgj", grad_grouped, full_down, preferred_element_type=jnp.float32
        )
        gelu_pull = jax.vjp(gelu_exact, up_proj)[1]
        grad_up = gelu_pull(grad_act)[0].astype(jnp.bfloat16)
        down_weight_grad = jnp.einsum(
            "rgi,rgj->igj", grad_grouped, activated, preferred_element_type=jnp.float32
        )
        up_weight_grad = jnp.einsum(
            "rgi,rgj->igj", rows_grouped, grad_up, preferred_element_type=jnp.float32
        )
        ffn_back = jnp.einsum(
            "rgj,igj->rgi", grad_up, full_up, preferred_element_type=jnp.float32
        ).reshape(piece_rows, D)
        grad_normed = grad_z + ffn_back
        grad_pre, gain_one_grad, bias_one_grad = norm_backward(
            grad_normed, normal_one, inverse_one, gain_one_f
        )
        grad_mix_low = grad_pre.astype(jnp.bfloat16)
        out_weight_grad = rows_product(context, grad_mix_low)
        grad_context = times_transposed(grad_mix_low, full_out).astype(jnp.bfloat16)
        grad_attn = grad_context[:, :attn_width]
        grad_heads = grad_attn.reshape(piece_rows, HEADS, HEAD_DIM)
        delta = delta_pass(
            heads_q,
            grad_heads,
            key_blocks,
            value_blocks,
            own_ids,
            id_blocks,
            log_total,
            score_scale,
        )
        grad_q_attn, all_kv_grads = full_grad_pass(
            heads_q,
            grad_heads,
            key_blocks,
            value_blocks,
            own_ids,
            id_blocks,
            log_total,
            delta,
            score_scale,
        )
        own_kv_grads = scatter_rows(all_kv_grads.astype(jnp.bfloat16), "ctx").astype(jnp.float32)
        grad_conv = (
            grad_context[:, attn_width:].astype(jnp.float32).reshape(piece_rows, HEADS, HEAD_DIM)
        )
        grad_taps = jnp.stack(
            [
                jnp.sum(grad_conv * ext_conv[j : j + piece_rows], axis=-1) * tap_mask[:, j : j + 1]
                for j in range(KERNEL)
            ],
            axis=-1,
        )
        grad_logits = (
            kernels * (grad_taps - jnp.sum(kernels * grad_taps, axis=-1, keepdims=True))
        ).reshape(piece_rows, HEADS * KERNEL)
        grad_conv_ext = sum(
            (
                jnp.pad(
                    kernels[:, :, j : j + 1] * tap_mask[:, j, None, None] * grad_conv,
                    ((j, 2 * radius - j), (0, 0), (0, 0)),
                )
                for j in range(KERNEL)
            )
        )
        grad_mixed_low = lax.optimization_barrier(
            jnp.dot(grad_logits, kernel_table.T, precision=HIGHEST).astype(jnp.bfloat16)
        )
        grad_mixed = grad_mixed_low.astype(jnp.float32)
        kernel_weight_grad = jnp.dot(
            mixed_low.astype(jnp.float32).T, grad_logits, precision=HIGHEST
        )
        grad_conv_key = (grad_mixed * query_f).astype(jnp.bfloat16)
        grad_q_total = grad_q_attn.reshape(piece_rows, attn_width) + grad_mixed * conv_key
        point_weight_grad = rows_product(pre_key_low, grad_conv_key)
        grad_pre_key = times_transposed(grad_conv_key, full_point)
        grad_tokens_ext = sum(
            (
                jnp.pad(
                    depth_table[:, j] * tap_mask[:, j : j + 1] * grad_pre_key,
                    ((j, 2 * radius - j), (0, 0)),
                )
                for j in range(KERNEL)
            )
        )
        depth_weight_grad = jnp.stack(
            [
                jnp.sum(
                    ext_tokens[j : j + piece_rows] * tap_mask[:, j : j + 1] * grad_pre_key, axis=0
                )
                for j in range(KERNEL)
            ],
            axis=1,
        )
        ext_grads = jnp.concatenate(
            [grad_tokens_ext, grad_conv_ext.reshape(piece_rows + 2 * radius, attn_width)], axis=1
        )
        rim_rows = jnp.concatenate([ext_grads[:radius], ext_grads[piece_rows + radius :]], axis=0)
        arrived = padded(rim_rows.astype(jnp.bfloat16), (("ctx", 0),), radius).astype(
            rim_rows.dtype
        )
        own_grads = ext_grads[radius : piece_rows + radius]
        own_grads = (
            own_grads.at[:radius]
            .add(arrived[:radius])
            .at[piece_rows - radius :]
            .add(arrived[3 * radius :])
        )
        grad_projected = jnp.concatenate(
            [grad_q_total, own_kv_grads, own_grads[:, D:]], axis=1
        ).astype(jnp.bfloat16)
        in_weight_grad = rows_product(tokens, grad_projected)
        input_grad = grad_pre + own_grads[:, :D] + times_transposed(grad_projected, full_in)
        input_grads.append(input_grad.astype(jnp.bfloat16))
        updates = (
            in_weight_grad,
            depth_weight_grad,
            point_weight_grad,
            kernel_weight_grad,
            out_weight_grad,
            gain_one_grad,
            bias_one_grad,
            gain_two_grad,
            bias_two_grad,
            up_weight_grad,
            down_weight_grad,
        )
        grad_totals = [running + change for running, change in zip(grad_totals, updates)]
    low_grads = [total.astype(jnp.bfloat16) for total in grad_totals]
    up_low, down_low = low_grads[9], low_grads[10]
    far_bits = [bit for bit in bits_of("ctx") if bit > 1]
    arrived = swap(jnp.where(on_high_core, up_low, down_low), "ctx", 1)
    block = jnp.where(on_high_core, down_low, up_low)
    block = (block.astype(jnp.float32) + arrived.astype(jnp.float32)).astype(jnp.bfloat16)
    block = fold(block, "dp", 1, 0)
    for bit in far_bits:
        block = fold(block, "ctx", bit, 0)
    columns = w_up.shape[2]
    lanes = len(bits_of("tensor"))
    block = block.reshape(block.shape[:2] + (2,) * lanes + (columns,))
    for step, bit in enumerate(bits_of("tensor")):
        block = fold(block, "tensor", bit, 2 + lanes - 1 - step)
        block = lax.squeeze(block, (2 + lanes - 1 - step,))
    for bit in reversed(far_bits):
        block = unfold(block, "ctx", bit, 0)
    other = swap(block, "ctx", 1)
    up_grad_out = jnp.where(on_high_core, other, block).astype(jnp.float32)
    down_grad_out = jnp.where(on_high_core, block, other).astype(jnp.float32)

    kernel_grad = low_grads[3]
    spread = jnp.zeros((D, HEADS * KERNEL), jnp.bfloat16)
    spread = spread.at[:kernel_rows].set(kernel_grad[:kernel_rows])
    spread = spread.at[half_rows : half_rows + kernel_rows].set(kernel_grad[kernel_rows:])
    small = fit(
        jnp.concatenate([low_grads[1], jnp.stack(low_grads[5:9], axis=1), spread], axis=1), D, 128
    )
    block = jnp.concatenate([low_grads[0], low_grads[4], low_grads[2], small], axis=1)
    steps = [("ctx", bit, 0) for bit in bits_of("ctx")]
    tensor_bits = bits_of("tensor")
    steps += [("tensor", bit, 1 if i == 0 else 0) for i, bit in enumerate(tensor_bits)]
    block = block.reshape(2, half_rows, -1)
    block = fold(block, "dp", 1, 0)[0]
    for axis, bit, dim in steps:
        block = fold(block, axis, bit, dim)
    for axis, bit, dim in reversed(steps):
        block = unfold(block, axis, bit, dim)
    block = block.astype(jnp.float32)
    in_width = w_in.shape[1]
    summed = [block[:, :in_width]]
    small = block[:, in_width + D + HEADS * HEAD_DIM :]
    summed.append(small[:, :KERNEL])
    summed.append(block[:, in_width + D : in_width + D + HEADS * HEAD_DIM])
    summed.append(small[:kernel_rows, KERNEL + 4 : KERNEL + 4 + HEADS * KERNEL])
    summed.append(block[:, in_width : in_width + D])
    summed += [small[:, KERNEL + i] for i in range(4)]
    layer_output = jnp.stack(outputs_list)[:, None]
    layer_input_grad = jnp.stack(input_grads)[:, None]
    return (
        layer_output,
        layer_input_grad,
        summed[0],
        summed[1],
        summed[2],
        summed[3],
        summed[4],
        summed[5],
        summed[6],
        summed[7],
        summed[8],
        up_grad_out,
        down_grad_out,
    )


def solution(mesh):
    return jax.shard_map(
        body,
        mesh=mesh,
        in_specs=(
            P(None, ("dp", "tensor"), "ctx", None),
            P(None, ("dp", "tensor"), None),
            P("dp", None),
            P("dp", None),
            P("dp", None),
            P("dp", None),
            P("dp", None),
            P("dp"),
            P("dp"),
            P("dp"),
            P("dp"),
            P("dp", None, "tensor"),
            P("dp", None, "tensor"),
            P(None, ("dp", "tensor"), "ctx", None),
        ),
        out_specs=(
            P(None, ("dp", "tensor"), "ctx", None),
            P(None, ("dp", "tensor"), "ctx", None),
            P("dp", None),
            P("dp", None),
            P("dp", None),
            P("dp", None),
            P("dp", None),
            P("dp"),
            P("dp"),
            P("dp"),
            P("dp"),
            P("dp", None, "tensor"),
            P("dp", None, "tensor"),
        ),
        check_vma=False,
    )
```

```python
import functools

import jax
import jax.numpy as jnp
from jax import lax
from jax.experimental import pallas as pl
from jax.experimental.pallas import tpu as pltpu
from jax.sharding import PartitionSpec as P

D = 768
HEADS = 6
HEAD_DIM = 64
KERNEL = 9
GROUPS = 2
MICRO = 2
WIDTH = HEADS * HEAD_DIM
PAIRS = HEADS // 2
RADIUS = KERNEL // 2
HALO = 16
SLOT = 8
LANES = 128
GROUP_WIDTH = D // GROUPS
NORM_EPS = 1e-05
NEG_FILL = -1e30
SCORE_SCALE = HEAD_DIM ** (-0.5)
F32 = jnp.float32
BF16 = jnp.bfloat16
VMEM_BYTES = 60 * 1024 * 1024


def nn(left, right):
    return lax.dot_general(left, right, (((1,), (0,)), ((), ())), preferred_element_type=F32)


def nt(left, right):
    return lax.dot_general(left, right, (((1,), (1,)), ((), ())), preferred_element_type=F32)


def tn(left, right):
    return lax.dot_general(left, right, (((0,), (0,)), ((), ())), preferred_element_type=F32)


def split(values):
    high = values.astype(BF16)
    return high, (values - high.astype(F32)).astype(BF16)


def rows_at(start, size, unit=16):
    return pl.ds(pl.multiple_of(start, unit), size)


def whole(shape):
    return pl.BlockSpec(shape, lambda *_: (0,) * len(shape))


def per_micro(shape):
    return pl.BlockSpec((None,) + shape, lambda m: (m,) + (0,) * len(shape))


SCALARS = pl.BlockSpec(memory_space=pltpu.SMEM)


def run(kernel, outs, args, specs=None, out_specs=None, grid=None, scratch=(), flops=0, name=None):
    moved = sum(a.size * a.dtype.itemsize for a in args) + sum(
        o.size * o.dtype.itemsize for o in outs
    )
    extra = {} if grid is None else {"grid": grid}
    if specs is None:
        specs = [SCALARS] + [pl.BlockSpec(memory_space=pltpu.VMEM)] * (len(args) - 1)
    if out_specs is None:
        out_specs = [pl.BlockSpec(memory_space=pltpu.VMEM)] * len(outs)
    return pl.pallas_call(
        kernel,
        out_shape=tuple(outs),
        in_specs=specs,
        out_specs=tuple(out_specs),
        scratch_shapes=list(scratch),
        compiler_params=pltpu.CompilerParams(vmem_limit_bytes=VMEM_BYTES),
        cost_estimate=pl.CostEstimate(flops=int(flops), bytes_accessed=moved, transcendentals=0),
        name=name,
        **extra,
    )(*args)


def shaped(shape, kind):
    return jax.ShapeDtypeStruct(shape, kind)


DP, CORE, YBIT, TENSOR, CTX = range(5)


def assemble(target, pos, own, mine, theirs):
    dp, core = pos[DP], pos[CORE]
    half, part = own.shape[0], mine.shape[0]
    target[rows_at(dp * half, half), :] = own
    target[rows_at((1 - dp) * half + core * part, part), :] = mine
    target[rows_at((1 - dp) * half + (1 - core) * part, part), :] = theirs


def kv_kernel(pos, tokens, own, mine, theirs, kv_out, w_out, table):
    assemble(w_out, pos, own[:, WIDTH : 3 * WIDTH], mine[...], theirs[...])

    def step(i, carry):
        rows = rows_at(i * 128, 128)
        kv_out[rows, :] = nn(tokens[rows, :], w_out[...]).astype(BF16)
        return carry

    lax.fori_loop(0, tokens.shape[0] // 128, step, 0)


def slot_max(values):
    for shift in (8, 16, 32, 64):
        values = jnp.maximum(values, pltpu.roll(values, shift, 1))
    return values


def slot_sum(values):
    for shift in (8, 16, 32, 64):
        values = values + pltpu.roll(values, shift, 1)
    return values


def tap_column(mask, j):
    return mask[:, SLOT * j : SLOT * j + 1]


def conv_kernel(
    pos, ext, mask, own_in, own_point, mine, theirs, taps, w_tap, spread,
    q_out, c_out, pre_out, key_out, mixed_out, kern_out, conv_out, w_qcp,
    ext_f, c_f, acc,
):
    rows = q_out.shape[0]
    span = ext.shape[0]

    @pl.when(pl.program_id(0) == 0)
    def _():
        assemble(w_qcp.at[:, :WIDTH], pos, own_in[:, :WIDTH], mine[:, :WIDTH], theirs[:, :WIDTH])
        assemble(
            w_qcp.at[:, WIDTH : 2 * WIDTH], pos, own_in[:, 3 * WIDTH :],
            mine[:, WIDTH : 2 * WIDTH], theirs[:, WIDTH : 2 * WIDTH],
        )
        assemble(
            w_qcp.at[:, 2 * WIDTH :], pos, own_point[...], mine[:, 2 * WIDTH :], theirs[:, 2 * WIDTH :]
        )

    ext_f[...] = ext[...].astype(F32)
    q = nn(ext[HALO : HALO + rows, :], w_qcp[:, :WIDTH]).astype(BF16)
    q_out[...] = q
    c_low = nn(ext[...], w_qcp[:, WIDTH : 2 * WIDTH]).astype(BF16)
    c_out[...] = c_low
    c_f[...] = c_low.astype(F32)

    def pre_step(i, carry):
        start = i * 64
        mask_rows = mask[rows_at(start, 64), :]
        for lane in range(0, D, 256):
            block = ext_f[rows_at(start + 8, 80, 8), lane : lane + 256]
            total = jnp.zeros((64, 256), F32)
            for j in range(KERNEL):
                total += block[RADIUS + j : RADIUS + j + 64, :] * taps[j : j + 1, lane : lane + 256] * tap_column(mask_rows, j)
            pre_out[rows_at(start, 64), lane : lane + 256] = total.astype(BF16)
        return carry

    lax.fori_loop(0, rows // 64, pre_step, 0)
    conv_key = nn(pre_out[...], w_qcp[:, 2 * WIDTH :])
    key_out[...] = conv_key
    mixed = (conv_key * q.astype(F32)).astype(BF16)
    mixed_out[...] = mixed
    logits = nn(mixed, w_tap[...])
    lane_id = lax.broadcasted_iota(jnp.int32, logits.shape, 1)
    logits = jnp.where(lane_id < SLOT * KERNEL, logits, NEG_FILL)
    expo = jnp.exp(logits - slot_max(logits))
    kern = expo / slot_sum(expo)
    kern_out[...] = kern
    high, low = split(kern * mask[...])
    both = jnp.concatenate([high, low], axis=1)
    for j in range(KERNEL):
        part = nn(both, spread[j]) * c_f[HALO - RADIUS + j : HALO - RADIUS + j + rows, :]
        if j == 0:
            acc[...] = part
        else:
            acc[...] += part
    conv_out[...] = acc[...].astype(BF16)


def attend_kernel(bounds, q, kv, key_ids, query_ids, context_out, out_t, lse_out, q_t, top, total, acc):
    micro = pl.program_id(0)
    block = q.shape[0]
    rows = q.shape[0]
    half = lax.broadcasted_iota(jnp.int32, (LANES, rows), 0) < HEAD_DIM
    scaled = q[...].astype(F32) * SCORE_SCALE
    for p in range(PAIRS):
        pair = jnp.transpose(scaled[:, p * LANES : (p + 1) * LANES])
        q_t[2 * p] = jnp.where(half, pair, 0.0).astype(BF16)
        q_t[2 * p + 1] = jnp.where(half, 0.0, pair).astype(BF16)
    top[...] = jnp.full_like(top, NEG_FILL)
    total[...] = jnp.zeros_like(total)
    acc[...] = jnp.zeros_like(acc)

    def step(b, carry):
        keys = rows_at(b * block, block)
        bias = jnp.where(key_ids[keys, :] == query_ids[...], 0.0, NEG_FILL)
        for h in range(HEADS):
            p = h // 2
            k_block = kv[keys, p * LANES : (p + 1) * LANES]
            v_block = kv[keys, WIDTH + p * LANES : WIDTH + (p + 1) * LANES]
            scores = nn(k_block, q_t[h]) + bias
            old = top[h : h + 1, :]
            new = jnp.maximum(old, jnp.max(scores, axis=0, keepdims=True))
            scale = jnp.exp(old - new)
            weights = jnp.exp(scores - new)
            total[h : h + 1, :] = total[h : h + 1, :] * scale + jnp.sum(weights, axis=0, keepdims=True)
            top[h : h + 1, :] = new
            part = tn(v_block, weights.astype(BF16))
            first = (h % 2) * HEAD_DIM
            own = slice(h * HEAD_DIM, (h + 1) * HEAD_DIM)
            acc[own, :] = acc[own, :] * scale + part[first : first + HEAD_DIM, :]
        return carry

    lax.fori_loop(bounds[0, micro], bounds[1, micro], step, 0)
    lse_out[...] = top[...] + jnp.log(jnp.maximum(total[...], 1e-37))
    for h in range(HEADS):
        own = slice(h * HEAD_DIM, (h + 1) * HEAD_DIM)
        out_t[own, :] = acc[own, :] / total[h : h + 1, :]
    for p in range(PAIRS):
        pair = slice(p * LANES, (p + 1) * LANES)
        context_out[:, pair] = jnp.transpose(out_t[pair, :]).astype(BF16)


def attend_back_kernel(
    bounds, pos, q, grad, kv, key_ids, query_ids, lse, out_t, dq_out, kv_grad,
    q_t, g_t, q_z, g_z, delta, acc,
):
    micro = pl.program_id(0)
    rows = q.shape[0]
    block = rows
    half = lax.broadcasted_iota(jnp.int32, (LANES, rows), 0) < HEAD_DIM
    half_lane = lax.broadcasted_iota(jnp.int32, (rows, LANES), 1) < HEAD_DIM
    for p in range(PAIRS):
        lanes = slice(p * LANES, (p + 1) * LANES)
        q_pair = q[:, lanes].astype(F32) * SCORE_SCALE
        g_pair = grad[:, lanes].astype(F32)
        for source, across, along in ((q_pair, q_t, q_z), (g_pair, g_t, g_z)):
            turned = jnp.transpose(source)
            across[2 * p] = jnp.where(half, turned, 0.0).astype(BF16)
            across[2 * p + 1] = jnp.where(half, 0.0, turned).astype(BF16)
            along[2 * p] = jnp.where(half_lane, source, 0.0).astype(BF16)
            along[2 * p + 1] = jnp.where(half_lane, 0.0, source).astype(BF16)
            if source is g_pair:
                product = turned * out_t[lanes, :]
                delta[2 * p : 2 * p + 1, :] = jnp.sum(product[:HEAD_DIM], axis=0, keepdims=True)
                delta[2 * p + 1 : 2 * p + 2, :] = jnp.sum(product[HEAD_DIM:], axis=0, keepdims=True)
    acc[...] = jnp.zeros_like(acc)
    kv_grad[...] = jnp.zeros_like(kv_grad)

    def step(b, carry):
        keys = rows_at(b * block, block)
        place = jnp.bitwise_xor(b, pos[CTX])
        near, far = place % 2, place // 2
        bias = jnp.where(key_ids[keys, :] == query_ids[...], 0.0, NEG_FILL)
        for p in range(PAIRS):
            lanes = slice(p * LANES, (p + 1) * LANES)
            k_block = kv[keys, lanes]
            v_block = kv[keys, WIDTH + p * LANES : WIDTH + (p + 1) * LANES]
            k_grad = v_grad = 0.0
            for h in (2 * p, 2 * p + 1):
                weights = jnp.exp(nn(k_block, q_t[h]) + bias - lse[h : h + 1, :])
                slopes = (weights * (nn(v_block, g_t[h]) - delta[h : h + 1, :])).astype(BF16)
                first = (h % 2) * HEAD_DIM
                own = slice(h * HEAD_DIM, (h + 1) * HEAD_DIM)
                acc[own, :] += tn(k_block, slopes)[first : first + HEAD_DIM, :]
                k_grad = k_grad + nn(slopes, q_z[h])
                v_grad = v_grad + nn(weights.astype(BF16), g_z[h])
            kv_grad[near, far, :, lanes] = k_grad.astype(BF16)
            kv_grad[near, far, :, WIDTH + p * LANES : WIDTH + (p + 1) * LANES] = v_grad.astype(BF16)
        return carry

    lax.fori_loop(bounds[0, micro], bounds[1, micro], step, 0)
    for p in range(PAIRS):
        pair = slice(p * LANES, (p + 1) * LANES)
        dq_out[:, pair] = jnp.transpose(acc[pair, :]) * SCORE_SCALE


def gelu_parts(values):
    spread = 0.5 * (1.0 + lax.erf(values * 0.7071067811865476))
    slope = spread + values * (jnp.exp(values * values * -0.5) * 0.3989422804014327)
    return values * spread, slope


def norm_stats(values):
    average = jnp.mean(values, axis=-1, keepdims=True)
    centred = values - average
    inverse = lax.rsqrt(jnp.mean(centred * centred, axis=-1, keepdims=True) + NORM_EPS)
    return centred * inverse, inverse


def norm_back(scaled, normal, inverse):
    inner = (
        scaled
        - jnp.mean(scaled, axis=-1, keepdims=True)
        - normal * jnp.mean(scaled * normal, axis=-1, keepdims=True)
    )
    return inner * inverse


def emit_rows(source, pos, keep, send):
    depth = keep.shape[3]
    for cc, target in ((0, keep), (1, send)):
        for dd in range(2):
            for yy in range(2):
                for k in range(keep.shape[2]):
                    start = (
                        jnp.bitwise_xor(pos[DP], dd) * (D // 2)
                        + jnp.bitwise_xor(pos[CORE], cc) * (D // 4)
                        + jnp.bitwise_xor(pos[YBIT], yy) * (D // 8)
                        + jnp.bitwise_xor(pos[TENSOR], k) * depth
                    )
                    target[dd, yy, k] = source[rows_at(start, depth, 8), :].astype(BF16)


ROWS_A = 256


def middle_kernel(
    pos, attn, conv, tokens, cotangent, own_out, mine_out, theirs_out, vectors,
    ffn_own, ffn_other, ffn_core_own, ffn_core_other,
    rows_out, pre_out, grad_attn, grad_conv, ffn_keep, ffn_send, out_keep, out_send, vector_grads,
    w_out, w_up, w_down, context, ffn_in, low_down, act, slope, grad_up, low_mix,
    normal, inverse, normed, total, out_grad,
):
    dp, core = pos[DP], pos[CORE]
    hidden = w_up.shape[2]
    shard = hidden // ffn_own.shape[0]
    half = GROUP_WIDTH // 2
    assemble(w_out, pos, own_out[...], mine_out[...], theirs_out[...])
    for gg, pair in ((0, (ffn_own, ffn_other)), (1, (ffn_core_own, ffn_core_other))):
        for dd in range(2):
            place = rows_at(jnp.bitwise_xor(dp, dd) * half, half)
            for k in range(ffn_own.shape[0]):
                columns = slice(k * shard, (k + 1) * shard)
                w_up[gg, place, columns] = pair[dd][k, 0]
                w_down[gg, place, columns] = pair[dd][k, 1]
    context[:, :WIDTH] = attn[...]
    context[:, WIDTH:] = conv[...]
    vector_grads[...] = jnp.zeros_like(vector_grads)
    gain_one, bias_one = vectors[0:1, :], vectors[1:2, :]
    gain_two, bias_two = vectors[2:3, :], vectors[3:4, :]
    group_of = [jnp.bitwise_xor(core, gg) * GROUP_WIDTH for gg in range(GROUPS)]

    def lanes_of(gg):
        return pl.ds(pl.multiple_of(group_of[gg], LANES), GROUP_WIDTH)

    def tile(i, carry):
        rows = rows_at(i * ROWS_A, ROWS_A)
        summed = tokens[rows, :].astype(F32) + nn(context[rows, :], w_out[...])
        normal_rows, inverse_rows = norm_stats(summed)
        normal[...] = normal_rows
        inverse[...] = inverse_rows
        normed_rows = normal_rows * gain_one + bias_one
        normed[...] = normed_rows
        ffn_in[rows, :] = normed_rows.astype(BF16)
        for gg in range(GROUPS):
            group_in = ffn_in[rows, lanes_of(gg)]

            def forward(k, carry):
                columns = pl.ds(pl.multiple_of(k * shard, LANES), shard)
                value, rate = gelu_parts(nn(group_in, w_up[gg, :, columns]))
                act[gg, rows, columns] = value.astype(BF16)
                slope[gg, :, columns] = rate
                return carry

            lax.fori_loop(0, hidden // shard, forward, 0)
            total[:, lanes_of(gg)] = normed[:, lanes_of(gg)] + nt(act[gg, rows, :], w_down[gg])
        normal_two, inverse_two = norm_stats(total[...])
        rows_out[rows, :] = (normal_two * gain_two + bias_two).astype(BF16)
        upstream = cotangent[rows, :].astype(F32)
        vector_grads[2:3, :] += jnp.sum(upstream * normal_two, axis=0, keepdims=True)
        vector_grads[3:4, :] += jnp.sum(upstream, axis=0, keepdims=True)
        grad_z = norm_back(upstream * gain_two, normal_two, inverse_two)
        total[...] = grad_z
        low_down[rows, :] = grad_z.astype(BF16)
        for gg in range(GROUPS):
            group_grad = low_down[rows, lanes_of(gg)]

            def backward(k, carry):
                columns = pl.ds(pl.multiple_of(k * shard, LANES), shard)
                grad = nn(group_grad, w_down[gg, :, columns]) * slope[gg, :, columns]
                grad_up[gg, rows, columns] = grad.astype(BF16)
                return carry

            lax.fori_loop(0, hidden // shard, backward, 0)
            total[:, lanes_of(gg)] += nt(grad_up[gg, rows, :], w_up[gg])
        grad_normed = total[...]
        vector_grads[0:1, :] += jnp.sum(grad_normed * normal[...], axis=0, keepdims=True)
        vector_grads[1:2, :] += jnp.sum(grad_normed, axis=0, keepdims=True)
        grad_pre = norm_back(grad_normed * gain_one, normal[...], inverse[...])
        pre_out[rows, :] = grad_pre
        low_mix[rows, :] = grad_pre.astype(BF16)
        grad_attn[rows, :] = nt(low_mix[rows, :], w_out[:WIDTH, :]).astype(BF16)
        grad_conv[rows, :] = nt(low_mix[rows, :], w_out[WIDTH:, :]).astype(BF16)
        return carry

    lax.fori_loop(0, tokens.shape[0] // ROWS_A, tile, 0)

    for gg, target in ((0, ffn_keep), (1, ffn_send)):

        def weights(k, carry):
            columns = pl.ds(pl.multiple_of(k * shard, LANES), shard)
            up_grad = tn(ffn_in[:, lanes_of(gg)], grad_up[gg, :, columns]).astype(BF16)
            down_grad = tn(low_down[:, lanes_of(gg)], act[gg, :, columns]).astype(BF16)
            for d in range(2):
                dd = jnp.bitwise_xor(dp, d)
                part = slice(d * half, (d + 1) * half)
                target[dd, pos[YBIT], k] = up_grad[part]
                target[dd, 1 - pos[YBIT], k] = down_grad[part]
            return carry

        lax.fori_loop(0, hidden // shard, weights, 0)
    out_grad[...] = tn(context[...], low_mix[...])
    emit_rows(out_grad, pos, out_keep, out_send)


def conv_back_kernel(
    grad_ext, kern_ext, c_ext, mask, mixed, q, conv_key, pre_key, ext, w_tap, w_qcp, spread,
    grad_c_out, dq_out, gpk_out, tap_grad, point_grad, depth_grad,
    grad_f, c_f, ext_f, prod, acc,
):
    rows = q.shape[0]
    own = slice(HALO, HALO + rows)

    @pl.when(pl.program_id(0) == 0)
    def _():
        tap_grad[...] = jnp.zeros_like(tap_grad)
        point_grad[...] = jnp.zeros_like(point_grad)
        depth_grad[...] = jnp.zeros_like(depth_grad)

    grad_f[...] = grad_ext[...].astype(F32)
    c_f[...] = c_ext[...].astype(F32)
    ext_f[...] = ext[...].astype(F32)
    taps = jnp.zeros((rows, LANES), F32)
    for j in range(KERNEL):
        shifted = slice(HALO - RADIUS + j, HALO - RADIUS + j + rows)
        taps += nt((grad_f[own, :] * c_f[shifted, :]).astype(BF16), spread[j, :LANES, :])
    taps = taps * mask[...]
    kern = kern_ext[own, :]
    grad_logits = kern * (taps - slot_sum(kern * taps))
    high, low = split(grad_logits)
    grad_mixed = (nt(high, w_tap[...]) + nt(low, w_tap[...])).astype(BF16).astype(F32)
    tap_grad[...] += tn(mixed[...], high) + tn(mixed[...], low)
    grad_key = (grad_mixed * q[...].astype(F32)).astype(BF16)
    dq_out[...] = grad_mixed * conv_key[...]
    point_grad[...] += tn(pre_key[...], grad_key)
    gpk_out[...] = nt(grad_key, w_qcp[:, 2 * WIDTH :])

    def depth_step(i, carry):
        start = i * 64
        mask_rows = mask[rows_at(start, 64), :]
        for lane in range(0, D, 256):
            lanes = slice(lane, lane + 256)
            block = ext_f[rows_at(start + 8, 80, 8), lanes]
            gpk = gpk_out[rows_at(start, 64), lanes]
            for j in range(KERNEL):
                value = block[RADIUS + j : RADIUS + j + 64, :] * (gpk * tap_column(mask_rows, j))
                depth_grad[j : j + 1, lanes] += jnp.sum(value, axis=0, keepdims=True)
        return carry

    lax.fori_loop(0, rows // 64, depth_step, 0)
    kern_high, kern_low = split(kern_ext[...])
    both = jnp.concatenate([kern_high, kern_low], axis=1)
    for j in range(KERNEL):
        prod[...] = nn(both, spread[KERNEL - 1 - j]) * grad_f[...]
        shifted = slice(HALO - RADIUS + j, HALO - RADIUS + j + rows)
        part = prod[shifted, :] * tap_column(mask[...], j)
        if j == 0:
            acc[...] = part
        else:
            acc[...] += part
    grad_c_out[...] = acc[...].astype(BF16)


def first_grads_kernel(
    pos, tokens, dq_attn, dq_conv, grad_c, point_grad, grad_q_out, keep, send, low_q, total
):
    low_q[...] = (dq_attn[...] + dq_conv[...]).astype(BF16)
    grad_q_out[...] = low_q[...]
    total[:, :WIDTH] = tn(tokens[...], low_q[...])
    total[:, WIDTH : 2 * WIDTH] = tn(tokens[...], grad_c[...])
    total[:, 2 * WIDTH :] = point_grad[...]
    emit_rows(total, pos, keep, send)


def second_grads_kernel(pos, tokens, kept, arrived, grad_kv_out, keep, send, low_kv, total):
    low_kv[...] = (kept[...].astype(F32) + arrived[...].astype(F32)).astype(BF16)
    grad_kv_out[...] = low_kv[...]
    total[...] = tn(tokens[...], low_kv[...])
    emit_rows(total, pos, keep, send)


def input_grad_kernel(
    pre, gpk, low_edge, high_edge, mask, taps, grad_q, grad_kv, grad_c, w_kv, w_qcp, out,
    gpk_ext, base,
):
    rows = gpk.shape[0]
    gpk_ext[:HALO, :] = low_edge[...].astype(F32)
    gpk_ext[HALO : HALO + rows, :] = gpk[...]
    gpk_ext[HALO + rows :, :] = high_edge[...].astype(F32)
    base[...] = (
        nt(grad_kv[...], w_kv[...])
        + nt(grad_q[...], w_qcp[:, :WIDTH])
        + nt(grad_c[...], w_qcp[:, WIDTH : 2 * WIDTH])
    )

    def step(i, carry):
        start = i * 64
        mask_rows = mask[rows_at(start, 64), :]
        for lane in range(0, D, 256):
            lanes = slice(lane, lane + 256)
            block = gpk_ext[rows_at(start + 8, 80, 8), lanes]
            place = rows_at(start, 64)
            value = base[place, lanes] + pre[place, lanes]
            for j in range(KERNEL):
                tap = taps[KERNEL - 1 - j : KERNEL - j, lanes]
                value += block[RADIUS + j : RADIUS + j + 64, :] * tap * tap_column(mask_rows, j)
            out[place, lanes] = value.astype(BF16)
        return carry

    lax.fori_loop(0, rows // 64, step, 0)


def unpack_kernel(pos, first_own, first_other, second_own, second_other, third_own, third_other,
                  in_out, out_out, point_out):
    depth = first_own.shape[2]
    for cc in range(2):
        for yy in range(2):
            for k in range(first_own.shape[1]):
                start = (
                    jnp.bitwise_xor(pos[CORE], cc) * (D // 4)
                    + jnp.bitwise_xor(pos[YBIT], yy) * (D // 8)
                    + jnp.bitwise_xor(pos[TENSOR], k) * depth
                )
                place = rows_at(start, depth, 8)
                first = (first_own, first_other)[cc][yy, k].astype(F32)
                second = (second_own, second_other)[cc][yy, k].astype(F32)
                third = (third_own, third_other)[cc][yy, k].astype(F32)
                out_out[place, :] = first
                in_out[place, :WIDTH] = second[:, :WIDTH]
                in_out[place, 3 * WIDTH :] = second[:, WIDTH : 2 * WIDTH]
                point_out[place, :] = second[:, 2 * WIDTH :]
                in_out[place, WIDTH : 3 * WIDTH] = third


def flips(axis, bit):
    return [(i, i ^ bit) for i in range(lax.axis_size(axis))]


def swap(block, axis, bit):
    return lax.ppermute(block, axis, flips(axis, bit))


def swap_both(block, bit):
    count = lax.axis_size("ctx")
    pairs = [
        (d * count + c, (1 - d) * count + (c ^ bit)) for d in range(2) for c in range(count)
    ]
    return lax.ppermute(block, ("dp", "ctx"), pairs)


def add_low(*blocks):
    return sum(b.astype(F32) for b in blocks).astype(BF16)


def far_bits():
    bits, bit = [], 4
    while bit < lax.axis_size("ctx"):
        bits.append(bit)
        bit *= 2
    return bits


def reduce_shares(keep, send):
    arrived = swap(send, "ctx", 1)
    part = {(d, y): add_low(keep[d, y], arrived[d, y]) for d in range(2) for y in range(2)}
    from_y = swap(part[0, 1], "ctx", 2)
    from_x = swap(part[1, 0], "dp", 1)
    from_xy = swap_both(part[1, 1], 2)
    count = keep.shape[2]
    slices = [
        add_low(part[0, 0][k], from_y[k], from_x[k], from_xy[k]) for k in range(count)
    ]
    share = add_low(slices[0], *[swap(slices[k], "tensor", k) for k in range(1, count)])
    for bit in far_bits():
        share = add_low(share, swap(share, "ctx", bit))
    return share


def gather_shares(share):
    count = lax.axis_size("tensor")
    stacked = jnp.stack([share] + [swap(share, "tensor", k) for k in range(1, count)])
    own = jnp.stack([stacked, swap(stacked, "ctx", 2)])
    return own, swap(own, "ctx", 1)


def neighbours(block):
    count = lax.axis_size("ctx")
    up = [(i, i + 1) for i in range(count - 1)]
    down = [(i + 1, i) for i in range(count - 1)]
    rows = block.shape[1]
    low = lax.ppermute(block[:, rows - HALO :], "ctx", up)
    high = lax.ppermute(block[:, :HALO], "ctx", down)
    return low, high


def with_edges(block, edges):
    return jnp.concatenate([edges[0], block, edges[1]], axis=1)


def ordered(own, other, high):
    return jnp.where(high, other, own), jnp.where(high, own, other)


def gather_kv(block):
    count, bit, depth = lax.axis_size("ctx"), lax.axis_size("ctx") // 2, 1
    index = lax.axis_index("ctx")
    micro, rows, width = block.shape
    while bit:
        other = swap(block, "ctx", bit)
        block = jnp.stack(ordered(block, other, (index // bit) % 2 == 1), axis=depth)
        depth += 1
        bit //= 2
    return block.reshape(micro, count * rows, width)


def body(
    hidden, segment_ids, w_in, w_depth, w_point, w_kernel, w_out,
    norm1_gain, norm1_bias, norm2_gain, norm2_bias, w_up, w_down, out_grad,
):
    micro, rows = MICRO, hidden.shape[2]
    seq = segment_ids.shape[2]
    flat = micro * rows
    ctx_count = lax.axis_size("ctx")
    tensor_count = lax.axis_size("tensor")
    dp, ctx, tensor = lax.axis_index("dp"), lax.axis_index("ctx"), lax.axis_index("tensor")
    core = ctx % 2
    pos = jnp.stack([dp, core, (ctx // 2) % 2, tensor, ctx]).astype(jnp.int32)
    tokens = hidden[:, 0]
    tokens_flat = tokens.reshape(flat, D)
    cotangent = out_grad[:, 0].reshape(flat, D)
    ids = segment_ids[:, 0]
    half = w_in.shape[0]
    part = half // 2
    depth_rows = D // 8 // tensor_count

    def part_of(weight):
        return lax.dynamic_slice_in_dim(weight, core * part, part, axis=0)

    kv_mine = swap(part_of(w_in[:, WIDTH : 3 * WIDTH]), "dp", 1)
    edges = neighbours(tokens)
    qcp_mine = swap(
        part_of(jnp.concatenate([w_in[:, :WIDTH], w_in[:, 3 * WIDTH :], w_point], axis=1)), "dp", 1
    )
    kv_theirs = swap(kv_mine, "ctx", 1)
    vectors = jnp.stack([norm1_gain, norm1_bias, norm2_gain, norm2_bias], axis=0)
    small = jnp.concatenate([w_depth.T, vectors], axis=0)
    small = jnp.pad(small, ((0, 16 - small.shape[0]), (0, 0)))
    tap_half = w_kernel.reshape(-1, HEADS, KERNEL).transpose(0, 2, 1)
    tap_half = jnp.pad(tap_half, ((0, 0), (0, 0), (0, SLOT - HEADS))).reshape(-1, SLOT * KERNEL)
    tap_half = jnp.pad(tap_half, ((0, 0), (0, LANES - SLOT * KERNEL)))
    small = jnp.concatenate(ordered(small, swap(small, "dp", 1), dp == 1), axis=1).astype(F32)
    w_tap = jnp.concatenate(ordered(tap_half, swap(tap_half, "dp", 1), dp == 1), axis=0)
    taps = jnp.pad(small[:KERNEL], ((0, 16 - KERNEL), (0, 0)))
    vectors = jnp.pad(small[KERNEL : KERNEL + 4], ((0, 4), (0, 0)))
    qcp_theirs = swap(qcp_mine, "ctx", 1)

    group = jnp.where(core == 1, jnp.stack([w_up[:, 1], w_down[:, 1]]), jnp.stack([w_up[:, 0], w_down[:, 0]]))
    ffn_own = jnp.stack([group] + [swap(group, "tensor", k) for k in range(1, tensor_count)])
    out_mine = swap(part_of(w_out), "dp", 1)
    out_theirs = swap(out_mine, "ctx", 1)
    ffn_other = swap(ffn_own, "dp", 1)
    ffn_core_own = swap(ffn_own, "ctx", 1)
    ffn_core_other = swap(ffn_other, "ctx", 1)

    offset = ctx * rows
    own_ids = lax.dynamic_slice_in_dim(ids, offset, rows, axis=1)
    window = lax.dynamic_slice_in_dim(
        jnp.pad(ids, ((0, 0), (RADIUS, RADIUS)), constant_values=-1), offset, rows + 2 * RADIUS, axis=1
    )
    mask = jnp.stack([window[:, j : j + rows] == own_ids for j in range(KERNEL)], axis=2)
    mask = jnp.broadcast_to(mask[..., None], mask.shape + (SLOT,)).reshape(micro, rows, SLOT * KERNEL)
    mask = jnp.pad(mask.astype(F32), ((0, 0), (0, 0), (0, LANES - SLOT * KERNEL)))
    blocks = ids.reshape(micro, ctx_count, rows)
    first = jnp.sum((blocks[:, :, -1] < own_ids[:, :1]).astype(jnp.int32), axis=1)
    last = jnp.sum((blocks[:, :, 0] <= own_ids[:, -1:]).astype(jnp.int32), axis=1)
    bounds = jnp.stack([first, last])
    key_ids = ids[:, :, None]
    query_ids = own_ids[:, None, :]
    lane_id = lax.broadcasted_iota(jnp.int32, (KERNEL, 2 * LANES, WIDTH), 1) % LANES
    head_id = lax.broadcasted_iota(jnp.int32, (KERNEL, 2 * LANES, WIDTH), 2) // HEAD_DIM
    tap_id = lax.broadcasted_iota(jnp.int32, (KERNEL, 2 * LANES, WIDTH), 0)
    spread = (lane_id == SLOT * tap_id + head_id).astype(BF16)

    kv_rows, w_kv = run(
        kv_kernel,
        [shaped((flat, 2 * WIDTH), BF16), shaped((D, 2 * WIDTH), BF16)],
        [pos, tokens_flat, w_in, kv_mine, kv_theirs],
        scratch=[pltpu.SMEM((1,), jnp.int32)],
        flops=2 * flat * D * 2 * WIDTH,
        name="kv",
    )
    kv = gather_kv(kv_rows.reshape(micro, rows, 2 * WIDTH))

    depth = {"pipeline_mode": pl.Buffered(1)} if seq > 2048 else {}

    def long_block(shape, index):
        return pl.BlockSpec(shape, index, **depth)

    seq_kv = long_block((None, seq, 2 * WIDTH), lambda m: (m, 0, 0))
    seq_ids = long_block((None, seq, 1), lambda m: (m, 0, 0))
    span = rows + 2 * HALO
    ext = with_edges(tokens, edges)
    once = whole
    q, c_ext, pre_key, conv_key, mixed, kern, conv_out, w_qcp = run(
        conv_kernel,
        [
            shaped((micro, rows, WIDTH), BF16), shaped((micro, span, WIDTH), BF16),
            shaped((micro, rows, D), BF16), shaped((micro, rows, WIDTH), F32),
            shaped((micro, rows, WIDTH), BF16), shaped((micro, rows, LANES), F32),
            shaped((micro, rows, WIDTH), BF16), shaped((D, 3 * WIDTH), BF16),
        ],
        [pos, ext, mask, w_in, w_point, qcp_mine, qcp_theirs, taps, w_tap, spread],
        specs=[SCALARS, per_micro((span, D)), per_micro((rows, LANES)), once(w_in.shape), once(w_point.shape),
               once(qcp_mine.shape), once(qcp_theirs.shape), once(taps.shape), once(w_tap.shape), once(spread.shape)],
        out_specs=[per_micro((rows, WIDTH)), per_micro((span, WIDTH)), per_micro((rows, D)), per_micro((rows, WIDTH)),
                   per_micro((rows, WIDTH)), per_micro((rows, LANES)), per_micro((rows, WIDTH)), once((D, 3 * WIDTH))],
        grid=(micro,),
        scratch=[pltpu.VMEM((span, D), F32), pltpu.VMEM((span, WIDTH), F32), pltpu.VMEM((rows, WIDTH), F32)],
        flops=2 * flat * WIDTH * (3 * D + 256 * KERNEL),
        name="conv",
    )
    kern_edges = neighbours(kern)

    head_scratch = pltpu.VMEM((HEADS, LANES, rows), BF16)
    lane_scratch = pltpu.VMEM((HEADS, rows, LANES), BF16)
    row_scratch = pltpu.VMEM((8, rows), F32)
    context, attn_t, lse = run(
        attend_kernel,
        [shaped((micro, rows, WIDTH), BF16), shaped((micro, WIDTH, rows), F32), shaped((micro, 8, rows), F32)],
        [bounds, q, kv, key_ids, query_ids],
        specs=[SCALARS, per_micro((rows, WIDTH)), seq_kv, seq_ids, per_micro((1, rows))],
        out_specs=[per_micro((rows, WIDTH)), per_micro((WIDTH, rows)), per_micro((8, rows))],
        grid=(micro,),
        scratch=[head_scratch, row_scratch, row_scratch, pltpu.VMEM((WIDTH, rows), F32)],
        flops=16 * flat * 4 * rows * WIDTH,
        name="attend",
    )

    hidden_units = tensor_count * w_up.shape[2]
    shard = w_up.shape[2]
    ffn_share = (2, 2, tensor_count, GROUP_WIDTH // 2, shard)

    def share(columns):
        return (2, 2, tensor_count, depth_rows, columns)

    rows_out, grad_pre, grad_attn, grad_conv, ffn_keep, ffn_send, out_keep, out_send, vector_grads = run(
        middle_kernel,
        [
            shaped((flat, D), BF16), shaped((flat, D), F32), shaped((flat, WIDTH), BF16), shaped((flat, WIDTH), BF16),
            shaped(ffn_share, BF16), shaped(ffn_share, BF16), shaped(share(D), BF16), shaped(share(D), BF16),
            shaped((8, D), F32),
        ],
        [pos, context.reshape(flat, WIDTH), conv_out.reshape(flat, WIDTH), tokens_flat, cotangent,
         w_out, out_mine, out_theirs, vectors, ffn_own, ffn_other, ffn_core_own, ffn_core_other],
        scratch=[
            pltpu.VMEM((D, D), BF16),
            pltpu.VMEM((GROUPS, GROUP_WIDTH, hidden_units), BF16),
            pltpu.VMEM((GROUPS, GROUP_WIDTH, hidden_units), BF16),
            pltpu.VMEM((flat, D), BF16), pltpu.VMEM((flat, D), BF16), pltpu.VMEM((flat, D), BF16),
            pltpu.VMEM((GROUPS, flat, hidden_units), BF16),
            pltpu.VMEM((GROUPS, ROWS_A, hidden_units), F32),
            pltpu.VMEM((GROUPS, flat, hidden_units), BF16),
            pltpu.VMEM((flat, D), BF16),
            pltpu.VMEM((ROWS_A, D), F32), pltpu.VMEM((ROWS_A, 1), F32),
            pltpu.VMEM((ROWS_A, D), F32), pltpu.VMEM((ROWS_A, D), F32), pltpu.VMEM((D, D), F32),
        ],
        flops=2 * flat * D * (3 * D + 3 * hidden_units),
        name="middle",
    )

    grad_attn = grad_attn.reshape(micro, rows, WIDTH)
    grad_conv = grad_conv.reshape(micro, rows, WIDTH)
    grad_ext = with_edges(grad_conv, neighbours(grad_conv))
    kern_ext = with_edges(kern, kern_edges)

    dq_attn, kv_grad = run(
        attend_back_kernel,
        [shaped((micro, rows, WIDTH), F32), shaped((2, ctx_count // 2, micro, rows, 2 * WIDTH), BF16)],
        [bounds, pos, q, grad_attn, kv, key_ids, query_ids, lse, attn_t],
        specs=[SCALARS, SCALARS, per_micro((rows, WIDTH)), per_micro((rows, WIDTH)), seq_kv,
               seq_ids, per_micro((1, rows)), per_micro((8, rows)), per_micro((WIDTH, rows))],
        out_specs=[per_micro((rows, WIDTH)),
                   long_block((2, ctx_count // 2, None, rows, 2 * WIDTH), lambda m: (0, 0, m, 0, 0))],
        grid=(micro,),
        scratch=[head_scratch, head_scratch, lane_scratch, lane_scratch, row_scratch, pltpu.VMEM((WIDTH, rows), F32)],
        flops=40 * flat * 4 * rows * WIDTH,
        name="attend_back",
    )
    arrived = swap(kv_grad[1], "ctx", 1)
    kv_parts = [add_low(kv_grad[0, k], arrived[k]) for k in range(ctx_count // 2)]
    bit = 2
    while len(kv_parts) > 2:
        received = swap(jnp.stack(kv_parts[1::2]), "ctx", bit)
        kv_parts = [add_low(a, received[k]) for k, a in enumerate(kv_parts[0::2])]
        bit *= 2
    kv_arrived = swap(kv_parts[1], "ctx", bit)

    grad_c, dq_conv, gpk, tap_grad, point_grad, depth_grad = run(
        conv_back_kernel,
        [
            shaped((micro, rows, WIDTH), BF16), shaped((micro, rows, WIDTH), F32), shaped((micro, rows, D), F32),
            shaped((WIDTH, LANES), F32), shaped((D, WIDTH), F32), shaped((16, D), F32),
        ],
        [grad_ext, kern_ext, c_ext, mask, mixed, q, conv_key, pre_key, ext, w_tap, w_qcp, spread],
        specs=[per_micro((span, WIDTH)), per_micro((span, LANES)), per_micro((span, WIDTH)), per_micro((rows, LANES)),
               per_micro((rows, WIDTH)), per_micro((rows, WIDTH)), per_micro((rows, WIDTH)), per_micro((rows, D)),
               per_micro((span, D)), once(w_tap.shape), once(w_qcp.shape), once(spread.shape)],
        out_specs=[per_micro((rows, WIDTH)), per_micro((rows, WIDTH)), per_micro((rows, D)),
                   once((WIDTH, LANES)), once((D, WIDTH)), once((16, D))],
        grid=(micro,),
        scratch=[pltpu.VMEM((span, WIDTH), F32), pltpu.VMEM((span, WIDTH), F32), pltpu.VMEM((span, D), F32),
                 pltpu.VMEM((span, WIDTH), F32), pltpu.VMEM((rows, WIDTH), F32)],
        flops=2 * flat * WIDTH * (3 * D + 512 * KERNEL),
        name="conv_back",
    )
    gpk_edges = neighbours(gpk.astype(BF16))

    wide = 3 * WIDTH
    grad_q, first_keep, first_send = run(
        first_grads_kernel,
        [shaped((flat, WIDTH), BF16), shaped(share(wide), BF16), shaped(share(wide), BF16)],
        [pos, tokens_flat, dq_attn.reshape(flat, WIDTH), dq_conv.reshape(flat, WIDTH),
         grad_c.reshape(flat, WIDTH), point_grad],
        scratch=[pltpu.VMEM((flat, WIDTH), BF16), pltpu.VMEM((D, wide), F32)],
        flops=2 * flat * D * 2 * WIDTH,
        name="first_grads",
    )
    grad_kv, second_keep, second_send = run(
        second_grads_kernel,
        [shaped((flat, 2 * WIDTH), BF16), shaped(share(2 * WIDTH), BF16), shaped(share(2 * WIDTH), BF16)],
        [pos, tokens_flat, kv_parts[0].reshape(flat, 2 * WIDTH), kv_arrived.reshape(flat, 2 * WIDTH)],
        scratch=[pltpu.VMEM((flat, 2 * WIDTH), BF16), pltpu.VMEM((D, 2 * WIDTH), F32)],
        flops=2 * flat * D * 2 * WIDTH,
        name="second_grads",
    )
    (input_grad,) = run(
        input_grad_kernel,
        [shaped((micro, rows, D), BF16)],
        [grad_pre.reshape(micro, rows, D), gpk, gpk_edges[0], gpk_edges[1], mask, taps,
         grad_q.reshape(micro, rows, WIDTH), grad_kv.reshape(micro, rows, 2 * WIDTH), grad_c, w_kv, w_qcp],
        specs=[per_micro((rows, D)), per_micro((rows, D)), per_micro((HALO, D)), per_micro((HALO, D)),
               per_micro((rows, LANES)), once(taps.shape), per_micro((rows, WIDTH)), per_micro((rows, 2 * WIDTH)),
               per_micro((rows, WIDTH)), once(w_kv.shape), once(w_qcp.shape)],
        out_specs=[per_micro((rows, D))],
        grid=(micro,),
        scratch=[pltpu.VMEM((span, D), F32), pltpu.VMEM((rows, D), F32)],
        flops=2 * flat * D * 4 * WIDTH,
        name="input_grad",
    )

    ffn_piece = reduce_shares(ffn_keep, ffn_send)
    ffn_pair = jnp.stack([ffn_piece, swap(ffn_piece, "ctx", 2)])
    ffn_far = swap(ffn_pair, "ctx", 1)
    on_y, on_core = (ctx // 2) % 2 == 1, core == 1
    groups = ordered(ffn_pair, ffn_far, on_core)
    up_parts, down_parts = zip(*[ordered(g[0], g[1], on_y) for g in groups])
    up_grad = jnp.stack(up_parts, axis=1).astype(F32)
    down_grad = jnp.stack(down_parts, axis=1).astype(F32)

    out_shares = gather_shares(reduce_shares(out_keep, out_send))
    first_shares = gather_shares(reduce_shares(first_keep, first_send))
    second_shares = gather_shares(reduce_shares(second_keep, second_send))
    in_grad, w_out_grad, w_point_grad = run(
        unpack_kernel,
        [shaped((half, 4 * WIDTH), F32), shaped((half, D), F32), shaped((half, WIDTH), F32)],
        [pos, *out_shares, *first_shares, *second_shares],
        name="unpack",
    )

    vector_half = D // 2
    packed = jnp.concatenate([depth_grad[:KERNEL], vector_grads[:4]], axis=0)
    packed = jnp.pad(packed, ((0, 16 - packed.shape[0]), (0, 0)))
    packed = jnp.concatenate(
        [packed.reshape(16, 2, vector_half).transpose(1, 0, 2).reshape(2, -1, LANES), tap_grad.reshape(2, -1, LANES)],
        axis=1,
    )
    sent = lax.dynamic_index_in_dim(packed, 1 - dp, 0, keepdims=False)
    packed = lax.dynamic_index_in_dim(packed, dp, 0, keepdims=False) + swap(sent, "dp", 1)
    bit = 1
    while bit < ctx_count:
        packed = packed + swap(packed, "ctx", bit)
        bit *= 2
    bit = 1
    while bit < tensor_count:
        packed = packed + swap(packed, "tensor", bit)
        bit *= 2
    rows_small = 16 * vector_half // LANES
    rest = packed[:rows_small].reshape(16, vector_half)
    tap_sum = packed[rows_small:][:, : SLOT * KERNEL].reshape(-1, KERNEL, SLOT)[:, :, :HEADS]
    tap_sum = tap_sum.transpose(0, 2, 1).reshape(-1, HEADS * KERNEL)

    return (
        rows_out.reshape(micro, 1, rows, D),
        input_grad[:, None],
        in_grad,
        rest[:KERNEL].T,
        w_point_grad,
        tap_sum,
        w_out_grad,
        rest[KERNEL],
        rest[KERNEL + 1],
        rest[KERNEL + 2],
        rest[KERNEL + 3],
        up_grad,
        down_grad,
    )


def solution(mesh):
    return jax.shard_map(
        body,
        mesh=mesh,
        in_specs=(
            P(None, ("dp", "tensor"), "ctx", None),
            P(None, ("dp", "tensor"), None),
            P("dp", None),
            P("dp", None),
            P("dp", None),
            P("dp", None),
            P("dp", None),
            P("dp"),
            P("dp"),
            P("dp"),
            P("dp"),
            P("dp", None, "tensor"),
            P("dp", None, "tensor"),
            P(None, ("dp", "tensor"), "ctx", None),
        ),
        out_specs=(
            P(None, ("dp", "tensor"), "ctx", None),
            P(None, ("dp", "tensor"), "ctx", None),
            P("dp", None),
            P("dp", None),
            P("dp", None),
            P("dp", None),
            P("dp", None),
            P("dp"),
            P("dp"),
            P("dp"),
            P("dp"),
            P("dp", None, "tensor"),
            P("dp", None, "tensor"),
        ),
        check_vma=False,
    )
```

```python
import jax
import jax.numpy as jnp
from jax import lax
from jax.experimental import pallas as pl
from jax.experimental.pallas import tpu as pltpu
from jax.sharding import PartitionSpec as P


D = 768
HEADS = 6
HEAD_DIM = 64
KERNEL = 9
GROUPS = 2
MICRO = 2
WIDTH = HEADS * HEAD_DIM
PAIRS = HEADS // 2
RADIUS = KERNEL // 2
HALO = 16
PAD = 8
ID_PAD = HALO + PAD
TILE = 32
SLOT = 8
LANES = 128
GROUP_WIDTH = D // GROUPS
NORM_EPS = 1e-05
NEG_FILL = -1e30
SCORE_SCALE = HEAD_DIM ** (-0.5)
F32 = jnp.float32
BF16 = jnp.bfloat16
VMEM_BYTES = 60 * 1024 * 1024


def nn(left, right):
    return lax.dot_general(left, right, (((1,), (0,)), ((), ())), preferred_element_type=F32)


def nt(left, right):
    return lax.dot_general(left, right, (((1,), (1,)), ((), ())), preferred_element_type=F32)


def tn(left, right):
    return lax.dot_general(left, right, (((0,), (0,)), ((), ())), preferred_element_type=F32)


def split(values):
    high = values.astype(BF16)
    return high, (values - high.astype(F32)).astype(BF16)


def rows_at(start, size, unit=16):
    return pl.ds(pl.multiple_of(start, unit), size)


def whole(shape):
    return pl.BlockSpec(shape, lambda *_: (0,) * len(shape))


def per_micro(shape):
    return pl.BlockSpec((None,) + shape, lambda m: (m,) + (0,) * len(shape))


SCALARS = pl.BlockSpec(memory_space=pltpu.SMEM)


def run(kernel, outs, args, specs=None, out_specs=None, grid=None, scratch=(), flops=0):
    moved = sum(a.size * a.dtype.itemsize for a in args) + sum(
        o.size * o.dtype.itemsize for o in outs
    )
    extra = {} if grid is None else {"grid": grid}
    if specs is None:
        specs = [SCALARS] + [pl.BlockSpec(memory_space=pltpu.VMEM)] * (len(args) - 1)
    if out_specs is None:
        out_specs = [pl.BlockSpec(memory_space=pltpu.VMEM)] * len(outs)
    return pl.pallas_call(
        kernel,
        out_shape=tuple(outs),
        in_specs=specs,
        out_specs=tuple(out_specs),
        scratch_shapes=list(scratch),
        compiler_params=pltpu.CompilerParams(vmem_limit_bytes=VMEM_BYTES),
        cost_estimate=pl.CostEstimate(flops=int(flops), bytes_accessed=moved, transcendentals=0),
        **extra,
    )(*args)


def shaped(shape, kind):
    return jax.ShapeDtypeStruct(shape, kind)


DP, CORE, YBIT, _, CTX = range(5)


def assemble(target, pos, own, mine, theirs):
    dp, core = pos[DP], pos[CORE]
    half, part = own.shape[0], mine.shape[0]
    target[rows_at(dp * half, half), :] = own
    target[rows_at((1 - dp) * half + core * part, part), :] = mine
    target[rows_at((1 - dp) * half + (1 - core) * part, part), :] = theirs


def kv_kernel(pos, tokens, own, mine, theirs, kv_out, w_out):
    assemble(w_out, pos, own[:, WIDTH : 3 * WIDTH], mine[...], theirs[...])

    def step(i, carry):
        rows = rows_at(i * 128, 128)
        kv_out[rows, :] = nn(tokens[rows, :], w_out[...]).astype(BF16)
        return carry

    lax.fori_loop(0, tokens.shape[0] // 128, step, 0)


def slot_max(values):
    for shift in (8, 16, 32, 64):
        values = jnp.maximum(values, pltpu.roll(values, shift, 1))
    return values


def slot_sum(values):
    for shift in (8, 16, 32, 64):
        values = values + pltpu.roll(values, shift, 1)
    return values


def tap_column(mask, j):
    return mask[:, SLOT * j : SLOT * j + 1]


def conv_kernel(
    pos, ext, ids, own_in, own_point, mine, theirs, taps, w_tap, spread,
    q_out, c_out, pre_out, key_out, mixed_out, kern_out, mask_out, conv_out, w_qcp,
    ext_f, c_f, acc, pre_all,
):
    span = ext.shape[0]
    rows = conv_out.shape[0]
    own = slice(HALO, HALO + rows)

    @pl.when(pl.program_id(0) == 0)
    def _():
        assemble(w_qcp.at[:, :WIDTH], pos, own_in[:, :WIDTH], mine[:, :WIDTH], theirs[:, :WIDTH])
        assemble(
            w_qcp.at[:, WIDTH : 2 * WIDTH], pos, own_in[:, 3 * WIDTH :],
            mine[:, WIDTH : 2 * WIDTH], theirs[:, WIDTH : 2 * WIDTH],
        )
        assemble(
            w_qcp.at[:, 2 * WIDTH :], pos, own_point[...],
            mine[:, 2 * WIDTH : 3 * WIDTH], theirs[:, 2 * WIDTH : 3 * WIDTH],
        )
        for padded in (ext_f, c_f):
            padded[:PAD, :] = jnp.zeros((PAD, padded.shape[1]), F32)
            padded[PAD + span :, :] = jnp.zeros((PAD, padded.shape[1]), F32)

    window = ids[rows_at(pos[CTX] * rows, span + 2 * PAD, 8), :]
    centre = window[PAD : PAD + span, :]
    slot_id = lax.broadcasted_iota(jnp.int32, (span, LANES), 1) // SLOT
    mask = jnp.zeros((span, LANES), F32)
    for j in range(KERNEL):
        same = jnp.where(window[PAD - RADIUS + j : PAD - RADIUS + j + span, :] == centre, 1.0, 0.0)
        mask = jnp.where(slot_id == j, same, mask)
    mask_out[...] = mask

    ext_f[PAD : PAD + span, :] = ext[...].astype(F32)
    q = nn(ext[...], w_qcp[:, :WIDTH]).astype(BF16)
    q_out[...] = q
    c_low = nn(ext[...], w_qcp[:, WIDTH : 2 * WIDTH]).astype(BF16)
    c_out[...] = c_low
    c_f[PAD : PAD + span, :] = c_low.astype(F32)

    def pre_step(i, carry):
        start = i * TILE
        mask_rows = mask_out[rows_at(start, TILE), :]
        for lane in range(0, D, WIDTH):
            lanes = slice(lane, lane + WIDTH)
            block = ext_f[rows_at(start, TILE + 2 * PAD, 8), lanes]
            total = jnp.zeros((TILE, WIDTH), F32)
            for j in range(KERNEL):
                first = PAD - RADIUS + j
                total += block[first : first + TILE, :] * taps[j : j + 1, lanes] * tap_column(mask_rows, j)
            pre_all[rows_at(start, TILE), lanes] = total.astype(BF16)
        return carry

    lax.fori_loop(0, span // TILE, pre_step, 0)
    pre_out[...] = pre_all[own, :]
    conv_key = nn(pre_all[...], w_qcp[:, 2 * WIDTH :])
    key_out[...] = conv_key[own, :]
    mixed = (conv_key * q.astype(F32)).astype(BF16)
    mixed_out[...] = mixed[own, :]
    logits = nn(mixed, w_tap[...])
    logits = jnp.where(slot_id < KERNEL, logits, NEG_FILL)
    expo = jnp.exp(logits - slot_max(logits))
    kern = expo / slot_sum(expo)
    kern_out[...] = kern
    high, low = split((kern * mask)[own, :])
    both = jnp.concatenate([high, low], axis=1)
    for j in range(KERNEL):
        first = PAD + HALO - RADIUS + j
        part = nn(both, spread[j]) * c_f[first : first + rows, :]
        if j == 0:
            acc[...] = part
        else:
            acc[...] += part
    conv_out[...] = acc[...].astype(BF16)


def kv_block(kv_near, kv_far, place):
    return jnp.where(place % 2 == 1, kv_far[place // 2], kv_near[place // 2])


def attend_kernel(
    bounds, pos, q_ext, kv_near, kv_far, key_ids, query_ids, context_out, out_t, lse_out,
    q_t, top, total, acc, kv,
):
    micro = pl.program_id(0)
    rows = context_out.shape[0]
    q = q_ext.at[HALO : HALO + rows, :]
    half = lax.broadcasted_iota(jnp.int32, (LANES, rows), 0) < HEAD_DIM
    scaled = q[...].astype(F32) * SCORE_SCALE
    for p in range(PAIRS):
        pair = jnp.transpose(scaled[:, p * LANES : (p + 1) * LANES])
        q_t[2 * p] = jnp.where(half, pair, 0.0).astype(BF16)
        q_t[2 * p + 1] = jnp.where(half, 0.0, pair).astype(BF16)
    top[...] = jnp.full_like(top, NEG_FILL)
    total[...] = jnp.zeros_like(total)
    acc[...] = jnp.zeros_like(acc)

    def step(b, carry):
        kv[...] = kv_block(kv_near, kv_far, jnp.bitwise_xor(b, pos[CTX]))
        bias = jnp.where(key_ids[rows_at(ID_PAD + b * rows, rows, 8), :] == query_ids[...], 0.0, NEG_FILL)
        for h in range(HEADS):
            p = h // 2
            k_block = kv[:, p * LANES : (p + 1) * LANES]
            v_block = kv[:, WIDTH + p * LANES : WIDTH + (p + 1) * LANES]
            scores = nn(k_block, q_t[h]) + bias
            old = top[h : h + 1, :]
            new = jnp.maximum(old, jnp.max(scores, axis=0, keepdims=True))
            scale = jnp.exp(old - new)
            weights = jnp.exp(scores - new)
            total[h : h + 1, :] = total[h : h + 1, :] * scale + jnp.sum(weights, axis=0, keepdims=True)
            top[h : h + 1, :] = new
            part = tn(v_block, weights.astype(BF16))
            first = (h % 2) * HEAD_DIM
            own = slice(h * HEAD_DIM, (h + 1) * HEAD_DIM)
            acc[own, :] = acc[own, :] * scale + part[first : first + HEAD_DIM, :]
        return carry

    lax.fori_loop(bounds[0, micro], bounds[1, micro], step, 0)
    lse_out[...] = top[...] + jnp.log(jnp.maximum(total[...], 1e-37))
    for h in range(HEADS):
        own = slice(h * HEAD_DIM, (h + 1) * HEAD_DIM)
        out_t[own, :] = acc[own, :] / total[h : h + 1, :]
    for p in range(PAIRS):
        pair = slice(p * LANES, (p + 1) * LANES)
        context_out[:, pair] = jnp.transpose(out_t[pair, :]).astype(BF16)


def attend_back_kernel(
    bounds, pos, q_ext, grad, kv_near, kv_far, key_ids, query_ids, lse, out_t, dq_out, grad_near, grad_far,
    q_t, g_t, q_z, g_z, delta, acc, kv,
):
    micro = pl.program_id(0)
    rows = grad.shape[0]
    q = q_ext.at[HALO : HALO + rows, :]
    half = lax.broadcasted_iota(jnp.int32, (LANES, rows), 0) < HEAD_DIM
    half_lane = lax.broadcasted_iota(jnp.int32, (rows, LANES), 1) < HEAD_DIM
    for p in range(PAIRS):
        lanes = slice(p * LANES, (p + 1) * LANES)
        q_pair = q[:, lanes].astype(F32) * SCORE_SCALE
        g_pair = grad[:, lanes].astype(F32)
        for source, across, along in ((q_pair, q_t, q_z), (g_pair, g_t, g_z)):
            turned = jnp.transpose(source)
            across[2 * p] = jnp.where(half, turned, 0.0).astype(BF16)
            across[2 * p + 1] = jnp.where(half, 0.0, turned).astype(BF16)
            along[2 * p] = jnp.where(half_lane, source, 0.0).astype(BF16)
            along[2 * p + 1] = jnp.where(half_lane, 0.0, source).astype(BF16)
            if source is g_pair:
                product = turned * out_t[lanes, :]
                delta[2 * p : 2 * p + 1, :] = jnp.sum(product[:HEAD_DIM], axis=0, keepdims=True)
                delta[2 * p + 1 : 2 * p + 2, :] = jnp.sum(product[HEAD_DIM:], axis=0, keepdims=True)
    acc[...] = jnp.zeros_like(acc)
    grad_near[...] = jnp.zeros_like(grad_near)
    grad_far[...] = jnp.zeros_like(grad_far)

    def step(b, carry):
        place = jnp.bitwise_xor(b, pos[CTX])
        kv[...] = kv_block(kv_near, kv_far, place)
        bias = jnp.where(key_ids[rows_at(ID_PAD + b * rows, rows, 8), :] == query_ids[...], 0.0, NEG_FILL)
        for p in range(PAIRS):
            lanes = slice(p * LANES, (p + 1) * LANES)
            value_lanes = slice(WIDTH + p * LANES, WIDTH + (p + 1) * LANES)
            k_block, v_block = kv[:, lanes], kv[:, value_lanes]
            k_grad = v_grad = 0.0
            for h in (2 * p, 2 * p + 1):
                weights = jnp.exp(nn(k_block, q_t[h]) + bias - lse[h : h + 1, :])
                slopes = (weights * (nn(v_block, g_t[h]) - delta[h : h + 1, :])).astype(BF16)
                first = (h % 2) * HEAD_DIM
                own = slice(h * HEAD_DIM, (h + 1) * HEAD_DIM)
                acc[own, :] += tn(k_block, slopes)[first : first + HEAD_DIM, :]
                k_grad = k_grad + nn(slopes, q_z[h])
                v_grad = v_grad + nn(weights.astype(BF16), g_z[h])
            kv[:, lanes] = k_grad.astype(BF16)
            kv[:, value_lanes] = v_grad.astype(BF16)

        @pl.when(place % 2 == 0)
        def _():
            grad_near[place // 2] = kv[...]

        @pl.when(place % 2 == 1)
        def _():
            grad_far[place // 2] = kv[...]

        return carry

    lax.fori_loop(bounds[0, micro], bounds[1, micro], step, 0)
    for p in range(PAIRS):
        pair = slice(p * LANES, (p + 1) * LANES)
        dq_out[:, pair] = jnp.transpose(acc[pair, :]) * SCORE_SCALE


def gelu_parts(values):
    spread = 0.5 * (1.0 + lax.erf(values * 0.7071067811865476))
    slope = spread + values * (jnp.exp(values * values * -0.5) * 0.3989422804014327)
    return values * spread, slope


def norm_stats(values):
    average = jnp.mean(values, axis=-1, keepdims=True)
    centred = values - average
    inverse = lax.rsqrt(jnp.mean(centred * centred, axis=-1, keepdims=True) + NORM_EPS)
    return centred * inverse, inverse


def norm_back(scaled, normal, inverse):
    inner = (
        scaled
        - jnp.mean(scaled, axis=-1, keepdims=True)
        - normal * jnp.mean(scaled * normal, axis=-1, keepdims=True)
    )
    return inner * inverse


def emit_rows(source, pos, keep, send):
    depth = D // 8
    for cc, target in ((0, keep), (1, send)):
        for dd in range(2):
            for yy in range(2):
                start = (
                    jnp.bitwise_xor(pos[DP], dd) * (D // 2)
                    + jnp.bitwise_xor(pos[CORE], cc) * (D // 4)
                    + jnp.bitwise_xor(pos[YBIT], yy) * depth
                )
                target[dd, yy, :depth] = source[rows_at(start, depth), :].astype(BF16)


ROWS_A = 256


def middle_kernel(
    pos, attn, conv, tokens, cotangent, own_out, mine_out, theirs_out, vectors, *rest
):
    ffn_parts, rest = rest[:8], rest[8:]
    rows_out, pre_out, grad_attn, grad_conv, ffn_keep, ffn_send, vector_grads = rest[:7]
    middle_steps(
        pos, attn, conv, tokens, cotangent, own_out, mine_out, theirs_out, vectors, ffn_parts,
        rows_out, pre_out, grad_attn, grad_conv, ffn_keep, ffn_send, vector_grads, *rest[7:]
    )


def middle_steps(
    pos, attn, conv, tokens, cotangent, own_out, mine_out, theirs_out, vectors, ffn_parts,
    rows_out, pre_out, grad_attn, grad_conv, ffn_keep, ffn_send, vector_grads,
    w_out, w_ffn, context, ffn_in, low_down, act, slope, grad_up, low_mix,
    normal, inverse, normed, total, out_grad,
):
    dp, core = pos[DP], pos[CORE]
    w_up, w_down = w_ffn.at[0], w_ffn.at[1]
    hidden = w_ffn.shape[3]
    shard = ffn_parts[0].shape[3]
    half = GROUP_WIDTH // 2
    low, high = 3 * WIDTH, 3 * WIDTH + D
    assemble(w_out, pos, own_out[...], mine_out[:, low:high], theirs_out[:, low:high])
    for gg in range(GROUPS):
        for dd in range(2):
            place = rows_at(jnp.bitwise_xor(dp, dd) * half, half)
            for part in range(2):
                piece = ffn_parts[4 * gg + 2 * dd + part]
                for k in range(piece.shape[0]):
                    first = (part * piece.shape[0] + k) * shard
                    for ud in range(2):
                        w_ffn[ud, gg, place, first : first + shard] = piece[k, ud]
    context[:, :WIDTH] = attn[...]
    context[:, WIDTH:] = conv[...]
    vector_grads[...] = jnp.zeros_like(vector_grads)
    gain_one, bias_one = vectors[0:1, :], vectors[1:2, :]
    gain_two, bias_two = vectors[2:3, :], vectors[3:4, :]
    group_of = [jnp.bitwise_xor(core, gg) * GROUP_WIDTH for gg in range(GROUPS)]

    def lanes_of(gg):
        return pl.ds(pl.multiple_of(group_of[gg], LANES), GROUP_WIDTH)

    def tile(i, carry):
        rows = rows_at(i * ROWS_A, ROWS_A)
        summed = tokens[rows, :].astype(F32) + nn(context[rows, :], w_out[...])
        normal_rows, inverse_rows = norm_stats(summed)
        normal[...] = normal_rows
        inverse[...] = inverse_rows
        normed_rows = normal_rows * gain_one + bias_one
        normed[...] = normed_rows
        ffn_in[rows, :] = normed_rows.astype(BF16)
        for gg in range(GROUPS):
            group_in = ffn_in[rows, lanes_of(gg)]

            def forward(k, carry):
                columns = pl.ds(pl.multiple_of(k * shard, LANES), shard)
                value, rate = gelu_parts(nn(group_in, w_up[gg, :, columns]))
                act[gg, rows, columns] = value.astype(BF16)
                slope[gg, :, columns] = rate
                return carry

            lax.fori_loop(0, hidden // shard, forward, 0)
            total[:, lanes_of(gg)] = normed[:, lanes_of(gg)] + nt(act[gg, rows, :], w_down[gg])
        normal_two, inverse_two = norm_stats(total[...])
        rows_out[rows, :] = (normal_two * gain_two + bias_two).astype(BF16)
        upstream = cotangent[rows, :].astype(F32)
        vector_grads[2:3, :] += jnp.sum(upstream * normal_two, axis=0, keepdims=True)
        vector_grads[3:4, :] += jnp.sum(upstream, axis=0, keepdims=True)
        grad_z = norm_back(upstream * gain_two, normal_two, inverse_two)
        total[...] = grad_z
        low_down[rows, :] = grad_z.astype(BF16)
        for gg in range(GROUPS):
            group_grad = low_down[rows, lanes_of(gg)]

            def backward(k, carry):
                columns = pl.ds(pl.multiple_of(k * shard, LANES), shard)
                grad = nn(group_grad, w_down[gg, :, columns]) * slope[gg, :, columns]
                grad_up[gg, rows, columns] = grad.astype(BF16)
                return carry

            lax.fori_loop(0, hidden // shard, backward, 0)
            total[:, lanes_of(gg)] += nt(grad_up[gg, rows, :], w_up[gg])
        grad_normed = total[...]
        vector_grads[0:1, :] += jnp.sum(grad_normed * normal[...], axis=0, keepdims=True)
        vector_grads[1:2, :] += jnp.sum(grad_normed, axis=0, keepdims=True)
        grad_pre = norm_back(grad_normed * gain_one, normal[...], inverse[...])
        pre_out[rows, :] = grad_pre
        low_mix[rows, :] = grad_pre.astype(BF16)
        grad_attn[rows, :] = nt(low_mix[rows, :], w_out[:WIDTH, :]).astype(BF16)
        grad_conv[rows, :] = nt(low_mix[rows, :], w_out[WIDTH:, :]).astype(BF16)
        return carry

    lax.fori_loop(0, tokens.shape[0] // ROWS_A, tile, 0)

    for gg, target in ((0, ffn_keep), (1, ffn_send)):

        def weights(k, carry):
            columns = pl.ds(pl.multiple_of(k * shard, LANES), shard)
            up_grad = tn(ffn_in[:, lanes_of(gg)], grad_up[gg, :, columns]).astype(BF16)
            down_grad = tn(low_down[:, lanes_of(gg)], act[gg, :, columns]).astype(BF16)
            for d in range(2):
                dd = jnp.bitwise_xor(dp, d)
                part = slice(d * half, (d + 1) * half)
                target[dd, pos[YBIT], k] = up_grad[part]
                target[dd, 1 - pos[YBIT], k] = down_grad[part]
            return carry

        lax.fori_loop(0, hidden // shard, weights, 0)
    out_grad[...] = tn(context[...], low_mix[...])
    last = hidden // shard
    for cc, target in ((0, ffn_keep), (1, ffn_send)):
        for dd in range(2):
            start = jnp.bitwise_xor(dp, dd) * (D // 2) + jnp.bitwise_xor(core, cc) * (D // 4)
            for yy in range(2):
                columns = pl.ds(
                    pl.multiple_of(jnp.bitwise_xor(pos[YBIT], yy) * (D // 2), LANES), D // 2
                )
                target[dd, yy, last] = out_grad[rows_at(start, D // 4), columns].astype(BF16)


def conv_back_kernel(
    grad_ext, kern_ext, c_ext, mask, mixed, q_ext, conv_key, pre_key, ext, pre_grad,
    w_tap, w_qcp, spread, tap_table,
    grad_c_out, dq_out, direct_out, tap_grad, point_grad, depth_grad,
    grad_f, c_f, ext_f, prod, acc, gpk_f,
):
    span = ext.shape[0]
    rows = mixed.shape[0]
    own = slice(HALO, HALO + rows)
    body = slice(PAD, PAD + span)

    @pl.when(pl.program_id(0) == 0)
    def _():
        tap_grad[...] = jnp.zeros_like(tap_grad)
        point_grad[...] = jnp.zeros_like(point_grad)
        depth_grad[...] = jnp.zeros_like(depth_grad)
        for padded in (grad_f, c_f, ext_f, prod, gpk_f):
            padded[:PAD, :] = jnp.zeros((PAD, padded.shape[1]), F32)
            padded[PAD + span :, :] = jnp.zeros((PAD, padded.shape[1]), F32)

    grad_f[body, :] = grad_ext[...].astype(F32)
    c_f[body, :] = c_ext[...].astype(F32)
    ext_f[body, :] = ext[...].astype(F32)
    taps = jnp.zeros((span, LANES), F32)
    for j in range(KERNEL):
        shifted = slice(PAD - RADIUS + j, PAD - RADIUS + j + span)
        taps += nt((grad_f[body, :] * c_f[shifted, :]).astype(BF16), spread[j, :LANES, :])
    taps = taps * mask[...]
    kern = kern_ext[...]
    grad_logits = kern * (taps - slot_sum(kern * taps))
    high, low = split(grad_logits)
    grad_mixed = (nt(high, w_tap[...]) + nt(low, w_tap[...])).astype(BF16).astype(F32)
    tap_grad[...] += tn(mixed[...], high[own, :]) + tn(mixed[...], low[own, :])
    grad_key = (grad_mixed * q_ext[...].astype(F32)).astype(BF16)
    dq_out[...] = grad_mixed[own, :] * conv_key[...]
    point_grad[...] += tn(pre_key[...], grad_key[own, :])
    gpk_f[body, :] = nt(grad_key, w_qcp[:, 2 * WIDTH :])

    def depth_step(i, carry):
        start = i * TILE
        place = rows_at(start, TILE)
        mask_rows = mask[rows_at(start + HALO, TILE), :]
        for lane in range(0, D, WIDTH):
            lanes = slice(lane, lane + WIDTH)
            block = ext_f[rows_at(start + HALO, TILE + 2 * PAD, 8), lanes]
            gpk_block = gpk_f[rows_at(start + HALO, TILE + 2 * PAD, 8), lanes]
            gpk = gpk_block[PAD : PAD + TILE, :]
            direct = pre_grad[place, lanes]
            for j in range(KERNEL):
                first = PAD - RADIUS + j
                column = tap_column(mask_rows, j)
                value = block[first : first + TILE, :] * (gpk * column)
                folded = value[0:8, :]
                for r in range(8, TILE, 8):
                    folded = folded + value[r : r + 8, :]
                depth_grad[8 * j : 8 * j + 8, lanes] += folded
                tap = tap_table[KERNEL - 1 - j : KERNEL - j, lanes]
                direct += gpk_block[first : first + TILE, :] * tap * column
            direct_out[place, lanes] = direct
        return carry

    lax.fori_loop(0, rows // TILE, depth_step, 0)
    kern_high, kern_low = split(kern)
    both = jnp.concatenate([kern_high, kern_low], axis=1)
    for j in range(KERNEL):
        prod[body, :] = nn(both, spread[KERNEL - 1 - j]) * grad_f[body, :]
        shifted = slice(PAD + HALO - RADIUS + j, PAD + HALO - RADIUS + j + rows)
        part = prod[shifted, :] * tap_column(mask[own, :], j)
        if j == 0:
            acc[...] = part
        else:
            acc[...] += part
    grad_c_out[...] = acc[...].astype(BF16)


EXTRA = 16
TAP_ROWS = 24


def first_grads_kernel(
    pos, tokens, dq_attn, dq_conv, grad_c, point_grad, depth_grad, vector_grads, tap_grad,
    grad_q_out, keep, send, low_q, total, extra,
):
    low_q[...] = (dq_attn[...] + dq_conv[...]).astype(BF16)
    grad_q_out[...] = low_q[...]
    total[:, :WIDTH] = tn(tokens[...], low_q[...])
    total[:, WIDTH : 2 * WIDTH] = tn(tokens[...], grad_c[...])
    total[:, 2 * WIDTH :] = point_grad[...]
    emit_rows(total, pos, keep, send)
    extra[...] = jnp.zeros_like(extra)
    half = D // 2
    for d in range(2):
        for i in range(WIDTH // 2 // TAP_ROWS):
            first = d * (WIDTH // 2) + i * TAP_ROWS
            extra[d, :TAP_ROWS, i * LANES : (i + 1) * LANES] = tap_grad[first : first + TAP_ROWS, :]
        lanes = slice(d * half, (d + 1) * half)
        for j in range(KERNEL):
            extra[d, TAP_ROWS + j : TAP_ROWS + j + 1, :half] = jnp.sum(
                depth_grad[8 * j : 8 * j + 8, lanes], axis=0, keepdims=True
            )
        extra[d, TAP_ROWS + KERNEL : TAP_ROWS + KERNEL + 4, :half] = vector_grads[:4, lanes]
    depth = D // 8
    for cc, target in ((0, keep), (1, send)):
        for dd in range(2):
            for yy in range(2):
                quarter = 2 * jnp.bitwise_xor(pos[CORE], cc) + jnp.bitwise_xor(pos[YBIT], yy)
                sheet = extra[jnp.bitwise_xor(pos[DP], dd), rows_at(quarter * EXTRA, EXTRA), :]
                target[dd, yy, depth:] = sheet.astype(BF16)


def second_grads_kernel(pos, tokens, kept, arrived, grad_kv_out, keep, send, low_kv, total):
    low_kv[...] = (kept[...].astype(F32) + arrived[...].astype(F32)).astype(BF16)
    grad_kv_out[...] = low_kv[...]
    total[...] = tn(tokens[...], low_kv[...])
    emit_rows(total, pos, keep, send)


def input_grad_kernel(direct, grad_q, grad_kv, grad_c, w_kv, w_qcp, out):
    value = direct[...] + nt(grad_q[...], w_qcp[:, :WIDTH])
    value += nt(grad_c[...], w_qcp[:, WIDTH : 2 * WIDTH])
    value += nt(grad_kv[...], w_kv[...])
    out[...] = value.astype(BF16)


def unpack_kernel(pos, f_own, f_other, first_own, first_other, second_own, second_other,
                  in_out, out_out, point_out, extra):
    depth = D // 8
    for cc in range(2):
        core = jnp.bitwise_xor(pos[CORE], cc)
        for yy in range(2):
            side = jnp.bitwise_xor(pos[YBIT], yy)
            place = rows_at(core * (D // 4) + side * depth, depth, 8)
            first = (first_own, first_other)[cc][yy].astype(F32)
            second = (second_own, second_other)[cc][yy].astype(F32)
            columns = pl.ds(pl.multiple_of(side * (D // 2), LANES), D // 2)
            out_out[rows_at(core * (D // 4), D // 4, 8), columns] = (f_own, f_other)[cc][yy, 1].astype(F32)
            in_out[place, :WIDTH] = first[:depth, :WIDTH]
            in_out[place, 3 * WIDTH :] = first[:depth, WIDTH : 2 * WIDTH]
            point_out[place, :] = first[:depth, 2 * WIDTH :]
            in_out[place, WIDTH : 3 * WIDTH] = second
            extra[rows_at((2 * core + side) * EXTRA, EXTRA, 8), :] = first[depth:, :]


def flips(axis, bit):
    return [(i, i ^ bit) for i in range(lax.axis_size(axis))]


def swap(block, axis, bit):
    return lax.ppermute(block, axis, flips(axis, bit))


def add_low(*blocks):
    return sum(b.astype(F32) for b in blocks).astype(BF16)


def far_bits():
    bits, bit = [], 4
    while bit < lax.axis_size("ctx"):
        bits.append(bit)
        bit *= 2
    return bits


def reduce_shares(keep, send):
    arrived = swap(send, "ctx", 1)
    sent = add_low(keep[1], arrived[1])
    received = swap(sent, "dp", 1)
    sent = add_low(keep[0, 1], arrived[0, 1], received[1])
    share = add_low(keep[0, 0], arrived[0, 0], received[0], swap(sent, "ctx", 2))
    for bit in far_bits():
        share = add_low(share, swap(share, "ctx", bit))
    return share


def reduce_line(share):
    bit = 1
    while bit < lax.axis_size("tensor"):
        share = add_low(share, swap(share, "tensor", bit))
        bit *= 2
    return share


def reduce_ffn(share):
    count, bit = lax.axis_size("tensor"), 1
    places = list(range(count))
    blocks = {k: share[k] for k in range(count + 1)}
    while bit < count:
        sent = jnp.stack([blocks[k] for k in places if k & bit] + [blocks[count]])
        received = swap(sent, "tensor", bit)
        kept = [k for k in places if not k & bit]
        blocks = {k: add_low(blocks[k], received[i]) for i, k in enumerate(kept + [count])}
        places = kept
        bit *= 2
    return jnp.stack([blocks[0], blocks[count]])


def gather_shares(share):
    own = jnp.stack([share, swap(share, "ctx", 2)])
    return own, swap(own, "ctx", 1)


def neighbours(block):
    count = lax.axis_size("ctx")
    up = [(i, i + 1) for i in range(count - 1)]
    down = [(i + 1, i) for i in range(count - 1)]
    rows = block.shape[1]
    low = lax.ppermute(block[:, rows - HALO :], "ctx", up)
    high = lax.ppermute(block[:, :HALO], "ctx", down)
    return low, high


def with_edges(block, edges):
    return jnp.concatenate([edges[0], block, edges[1]], axis=1)


def ordered(own, other, high):
    return jnp.where(high, other, own), jnp.where(high, own, other)


def gather_kv(block):
    block, bit = block[None], 2
    while bit < lax.axis_size("ctx"):
        block = jnp.concatenate([block, swap(block, "ctx", bit)], axis=0)
        bit *= 2
    return block, swap(block, "ctx", 1)


def layer(
    hidden, segment_ids, w_in, w_depth, w_point, w_kernel, w_out,
    norm1_gain, norm1_bias, norm2_gain, norm2_bias, w_up, w_down, out_grad,
):
    micro, rows = MICRO, hidden.shape[2]
    seq = segment_ids.shape[2]
    flat = micro * rows
    ctx_count = lax.axis_size("ctx")
    tensor_count = lax.axis_size("tensor")
    dp, ctx, tensor = lax.axis_index("dp"), lax.axis_index("ctx"), lax.axis_index("tensor")
    core = ctx % 2
    pos = jnp.stack([dp, core, (ctx // 2) % 2, tensor, ctx]).astype(jnp.int32)
    tokens = hidden[:, 0]
    tokens_flat = tokens.reshape(flat, D)
    cotangent = out_grad[:, 0].reshape(flat, D)
    ids = segment_ids[:, 0]
    half = w_in.shape[0]
    part = half // 2

    def part_of(weight):
        return lax.dynamic_slice_in_dim(weight, core * part, part, axis=0)

    kv_mine = swap(part_of(w_in)[:, WIDTH : 3 * WIDTH], "dp", 1)
    edges = neighbours(tokens)
    vectors = jnp.stack([norm1_gain, norm1_bias, norm2_gain, norm2_bias], axis=0)
    small = jnp.concatenate([w_depth.T, vectors], axis=0)
    small = jnp.pad(small, ((0, 16 - small.shape[0]), (0, 0)))
    tap_half = w_kernel.reshape(-1, HEADS, KERNEL).transpose(0, 2, 1)
    tap_half = jnp.pad(tap_half, ((0, 0), (0, 0), (0, SLOT - HEADS))).reshape(-1, SLOT * KERNEL)
    tap_half = jnp.pad(tap_half, ((0, 0), (0, LANES - SLOT * KERNEL)))
    sheet = small.reshape(-1, LANES)
    sheet = jnp.pad(sheet, ((0, part - sheet.shape[0]), (0, 0)))
    own_part = part_of(w_in)
    pack = jnp.concatenate(
        [own_part[:, :WIDTH], own_part[:, 3 * WIDTH :], part_of(w_point), part_of(w_out),
         jnp.where(core == 1, sheet, tap_half)],
        axis=1,
    )
    pack_mine = swap(pack, "dp", 1)
    kv_theirs = swap(kv_mine, "ctx", 1)
    pack_theirs = swap(pack_mine, "ctx", 1)
    tap_other, small_other = ordered(pack_mine[:, 3 * WIDTH + D :], pack_theirs[:, 3 * WIDTH + D :], core == 1)
    small_other = small_other[: 16 * half // LANES].reshape(16, half)
    small = jnp.concatenate(ordered(small, small_other, dp == 1), axis=1).astype(F32)
    w_tap = jnp.concatenate(ordered(tap_half, tap_other, dp == 1), axis=0)
    taps = small
    vectors = small[KERNEL : KERNEL + 4]

    def side(weight):
        return jnp.where(core == 1, weight[:, 1], weight[:, 0])

    ffn, bit = jnp.stack([side(w_up), side(w_down)])[None], 1
    while 2 * bit < tensor_count:
        ffn = jnp.concatenate([ffn, swap(ffn, "tensor", bit)], axis=0)
        bit *= 2
    ffn_parts = [ffn, swap(ffn, "tensor", bit)]
    ffn_parts += [swap(piece, "dp", 1) for piece in ffn_parts]
    ffn_parts += [swap(piece, "ctx", 1) for piece in ffn_parts]

    offset = ctx * rows
    own_ids = lax.dynamic_slice_in_dim(ids, offset, rows, axis=1)
    blocks = ids.reshape(micro, ctx_count, rows)
    first = jnp.sum((blocks[:, :, -1] < own_ids[:, :1]).astype(jnp.int32), axis=1)
    last = jnp.sum((blocks[:, :, 0] <= own_ids[:, -1:]).astype(jnp.int32), axis=1)
    bounds = jnp.stack([first, last])
    key_ids = jnp.pad(ids, ((0, 0), (ID_PAD, ID_PAD)), constant_values=-1)[:, :, None]
    query_ids = own_ids[:, None, :]
    lane_id = lax.broadcasted_iota(jnp.int32, (KERNEL, 2 * LANES, WIDTH), 1) % LANES
    head_id = lax.broadcasted_iota(jnp.int32, (KERNEL, 2 * LANES, WIDTH), 2) // HEAD_DIM
    tap_id = lax.broadcasted_iota(jnp.int32, (KERNEL, 2 * LANES, WIDTH), 0)
    spread = (lane_id == SLOT * tap_id + head_id).astype(BF16)

    kv_rows, w_kv = run(
        kv_kernel,
        [shaped((flat, 2 * WIDTH), BF16), shaped((D, 2 * WIDTH), BF16)],
        [pos, tokens_flat, w_in, kv_mine, kv_theirs],
        flops=2 * flat * D * 2 * WIDTH,
    )
    kv_near, kv_far = gather_kv(kv_rows.reshape(micro, rows, 2 * WIDTH))

    depth = {"pipeline_mode": pl.Buffered(1)} if seq > 2048 else {}

    def long_block(shape, index):
        return pl.BlockSpec(shape, index, **depth)

    kv_half = long_block((ctx_count // 2, None, rows, 2 * WIDTH), lambda m: (0, m, 0, 0))
    seq_ids = long_block((None, seq + 2 * ID_PAD, 1), lambda m: (m, 0, 0))
    span = rows + 2 * HALO
    ext = with_edges(tokens, edges)
    once = whole
    q_ext, c_ext, pre_key, conv_key, mixed, kern_ext, mask, conv_out, w_qcp = run(
        conv_kernel,
        [
            shaped((micro, span, WIDTH), BF16), shaped((micro, span, WIDTH), BF16),
            shaped((micro, rows, D), BF16), shaped((micro, rows, WIDTH), F32),
            shaped((micro, rows, WIDTH), BF16), shaped((micro, span, LANES), F32), shaped((micro, span, LANES), F32),
            shaped((micro, rows, WIDTH), BF16), shaped((D, 3 * WIDTH), BF16),
        ],
        [pos, ext, key_ids, w_in, w_point, pack_mine, pack_theirs, taps, w_tap, spread],
        specs=[SCALARS, per_micro((span, D)), seq_ids, once(w_in.shape), once(w_point.shape),
               once(pack_mine.shape), once(pack_theirs.shape), once(taps.shape), once(w_tap.shape), once(spread.shape)],
        out_specs=[per_micro((span, WIDTH)), per_micro((span, WIDTH)), per_micro((rows, D)), per_micro((rows, WIDTH)),
                   per_micro((rows, WIDTH)), per_micro((span, LANES)), per_micro((span, LANES)),
                   per_micro((rows, WIDTH)), once((D, 3 * WIDTH))],
        grid=(micro,),
        scratch=[pltpu.VMEM((span + 2 * PAD, D), F32), pltpu.VMEM((span + 2 * PAD, WIDTH), F32),
                 pltpu.VMEM((rows, WIDTH), F32), pltpu.VMEM((span, D), BF16)],
        flops=2 * flat * WIDTH * (3 * D + 256 * KERNEL),
    )

    head_scratch = pltpu.VMEM((HEADS, LANES, rows), BF16)
    lane_scratch = pltpu.VMEM((HEADS, rows, LANES), BF16)
    row_scratch = pltpu.VMEM((8, rows), F32)
    block_scratch = pltpu.VMEM((rows, 2 * WIDTH), BF16)
    context, attn_t, lse = run(
        attend_kernel,
        [shaped((micro, rows, WIDTH), BF16), shaped((micro, WIDTH, rows), F32), shaped((micro, 8, rows), F32)],
        [bounds, pos, q_ext, kv_near, kv_far, key_ids, query_ids],
        specs=[SCALARS, SCALARS, per_micro((span, WIDTH)), kv_half, kv_half, seq_ids, per_micro((1, rows))],
        out_specs=[per_micro((rows, WIDTH)), per_micro((WIDTH, rows)), per_micro((8, rows))],
        grid=(micro,),
        scratch=[head_scratch, row_scratch, row_scratch, pltpu.VMEM((WIDTH, rows), F32), block_scratch],
        flops=16 * flat * 4 * rows * WIDTH,
    )

    hidden_units = tensor_count * w_up.shape[2]
    shard = w_up.shape[2]
    ffn_share = (2, 2, tensor_count + 1, GROUP_WIDTH // 2, shard)

    rows_out, grad_pre, grad_attn, grad_conv, ffn_keep, ffn_send, vector_grads = run(
        middle_kernel,
        [
            shaped((flat, D), BF16), shaped((flat, D), F32), shaped((flat, WIDTH), BF16), shaped((flat, WIDTH), BF16),
            shaped(ffn_share, BF16), shaped(ffn_share, BF16),
            shaped((8, D), F32),
        ],
        [pos, context.reshape(flat, WIDTH), conv_out.reshape(flat, WIDTH), tokens_flat, cotangent,
         w_out, pack_mine, pack_theirs, vectors, *ffn_parts],
        scratch=[
            pltpu.VMEM((D, D), BF16),
            pltpu.VMEM((2, GROUPS, GROUP_WIDTH, hidden_units), BF16),
            pltpu.VMEM((flat, D), BF16), pltpu.VMEM((flat, D), BF16), pltpu.VMEM((flat, D), BF16),
            pltpu.VMEM((GROUPS, flat, hidden_units), BF16),
            pltpu.VMEM((GROUPS, ROWS_A, hidden_units), F32),
            pltpu.VMEM((GROUPS, flat, hidden_units), BF16),
            pltpu.VMEM((flat, D), BF16),
            pltpu.VMEM((ROWS_A, D), F32), pltpu.VMEM((ROWS_A, 1), F32),
            pltpu.VMEM((ROWS_A, D), F32), pltpu.VMEM((ROWS_A, D), F32), pltpu.VMEM((D, D), F32),
        ],
        flops=2 * flat * D * (3 * D + 3 * hidden_units),
    )

    grad_attn = grad_attn.reshape(micro, rows, WIDTH)
    grad_conv = grad_conv.reshape(micro, rows, WIDTH)
    grad_ext = with_edges(grad_conv, neighbours(grad_conv))

    dq_attn, grad_near, grad_far = run(
        attend_back_kernel,
        [shaped((micro, rows, WIDTH), F32), shaped((ctx_count // 2, micro, rows, 2 * WIDTH), BF16),
         shaped((ctx_count // 2, micro, rows, 2 * WIDTH), BF16)],
        [bounds, pos, q_ext, grad_attn, kv_near, kv_far, key_ids, query_ids, lse, attn_t],
        specs=[SCALARS, SCALARS, per_micro((span, WIDTH)), per_micro((rows, WIDTH)), kv_half, kv_half,
               seq_ids, per_micro((1, rows)), per_micro((8, rows)), per_micro((WIDTH, rows))],
        out_specs=[per_micro((rows, WIDTH)), kv_half, kv_half],
        grid=(micro,),
        scratch=[head_scratch, head_scratch, lane_scratch, lane_scratch, row_scratch,
                 pltpu.VMEM((WIDTH, rows), F32), block_scratch],
        flops=40 * flat * 4 * rows * WIDTH,
    )
    arrived = swap(grad_far, "ctx", 1)
    kv_parts = [add_low(grad_near[k], arrived[k]) for k in range(ctx_count // 2)]
    bit = 2
    while len(kv_parts) > 2:
        received = swap(jnp.stack(kv_parts[1::2]), "ctx", bit)
        kv_parts = [add_low(a, received[k]) for k, a in enumerate(kv_parts[0::2])]
        bit *= 2
    kv_arrived = swap(kv_parts[1], "ctx", bit)

    grad_c, dq_conv, direct, tap_grad, point_grad, depth_grad = run(
        conv_back_kernel,
        [
            shaped((micro, rows, WIDTH), BF16), shaped((micro, rows, WIDTH), F32), shaped((micro, rows, D), F32),
            shaped((WIDTH, LANES), F32), shaped((D, WIDTH), F32), shaped((8 * KERNEL, D), F32),
        ],
        [grad_ext, kern_ext, c_ext, mask, mixed, q_ext, conv_key, pre_key, ext, grad_pre.reshape(micro, rows, D),
         w_tap, w_qcp, spread, taps],
        specs=[per_micro((span, WIDTH)), per_micro((span, LANES)), per_micro((span, WIDTH)), per_micro((span, LANES)),
               per_micro((rows, WIDTH)), per_micro((span, WIDTH)), per_micro((rows, WIDTH)), per_micro((rows, D)),
               per_micro((span, D)), per_micro((rows, D)), once(w_tap.shape), once(w_qcp.shape), once(spread.shape),
               once(taps.shape)],
        out_specs=[per_micro((rows, WIDTH)), per_micro((rows, WIDTH)), per_micro((rows, D)),
                   once((WIDTH, LANES)), once((D, WIDTH)), once((8 * KERNEL, D))],
        grid=(micro,),
        scratch=[pltpu.VMEM((span + 2 * PAD, WIDTH), F32), pltpu.VMEM((span + 2 * PAD, WIDTH), F32),
                 pltpu.VMEM((span + 2 * PAD, D), F32), pltpu.VMEM((span + 2 * PAD, WIDTH), F32),
                 pltpu.VMEM((rows, WIDTH), F32), pltpu.VMEM((span + 2 * PAD, D), F32)],
        flops=2 * flat * WIDTH * (3 * D + 512 * KERNEL),
    )

    wide = 3 * WIDTH
    depth = D // 8
    first_share = shaped((2, 2, depth + EXTRA, wide), BF16)
    grad_q, first_keep, first_send = run(
        first_grads_kernel,
        [shaped((flat, WIDTH), BF16), first_share, first_share],
        [pos, tokens_flat, dq_attn.reshape(flat, WIDTH), dq_conv.reshape(flat, WIDTH),
         grad_c.reshape(flat, WIDTH), point_grad, depth_grad, vector_grads, tap_grad],
        scratch=[pltpu.VMEM((flat, WIDTH), BF16), pltpu.VMEM((D, wide), F32), pltpu.VMEM((2, 4 * EXTRA, wide), F32)],
        flops=2 * flat * D * 2 * WIDTH,
    )
    second_share = shaped((2, 2, depth, 2 * WIDTH), BF16)
    grad_kv, second_keep, second_send = run(
        second_grads_kernel,
        [shaped((flat, 2 * WIDTH), BF16), second_share, second_share],
        [pos, tokens_flat, kv_parts[0].reshape(flat, 2 * WIDTH), kv_arrived.reshape(flat, 2 * WIDTH)],
        scratch=[pltpu.VMEM((flat, 2 * WIDTH), BF16), pltpu.VMEM((D, 2 * WIDTH), F32)],
        flops=2 * flat * D * 2 * WIDTH,
    )
    (input_grad,) = run(
        input_grad_kernel,
        [shaped((micro, rows, D), BF16)],
        [direct, grad_q.reshape(micro, rows, WIDTH), grad_kv.reshape(micro, rows, 2 * WIDTH), grad_c, w_kv, w_qcp],
        specs=[per_micro((rows, D)), per_micro((rows, WIDTH)), per_micro((rows, 2 * WIDTH)),
               per_micro((rows, WIDTH)), once(w_kv.shape), once(w_qcp.shape)],
        out_specs=[per_micro((rows, D))],
        grid=(micro,),
        flops=2 * flat * D * 4 * WIDTH,
    )

    f_own, f_other = gather_shares(reduce_ffn(reduce_shares(ffn_keep, ffn_send)))
    groups = ordered(f_own[:, 0], f_other[:, 0], core == 1)
    up_parts, down_parts = zip(*[ordered(g[0], g[1], (ctx // 2) % 2 == 1) for g in groups])
    up_grad = jnp.stack(up_parts, axis=1).astype(F32)
    down_grad = jnp.stack(down_parts, axis=1).astype(F32)
    first_shares = gather_shares(reduce_line(reduce_shares(first_keep, first_send)))
    second_shares = gather_shares(reduce_line(reduce_shares(second_keep, second_send)))
    in_grad, w_out_grad, w_point_grad, extra = run(
        unpack_kernel,
        [shaped((half, 4 * WIDTH), F32), shaped((half, D), F32), shaped((half, WIDTH), F32),
         shaped((4 * EXTRA, wide), F32)],
        [pos, f_own, f_other, *first_shares, *second_shares],
    )
    tap_sum = extra[:TAP_ROWS, : WIDTH // 2 // TAP_ROWS * LANES].reshape(TAP_ROWS, -1, LANES)
    tap_sum = tap_sum.transpose(1, 0, 2).reshape(WIDTH // 2, LANES)[:, : SLOT * KERNEL]
    tap_sum = tap_sum.reshape(-1, KERNEL, SLOT)[:, :, :HEADS].transpose(0, 2, 1).reshape(-1, HEADS * KERNEL)
    rest = extra[TAP_ROWS : TAP_ROWS + 16, :half]

    return (
        rows_out.reshape(micro, 1, rows, D),
        input_grad[:, None],
        in_grad,
        rest[:KERNEL].T,
        w_point_grad,
        tap_sum,
        w_out_grad,
        rest[KERNEL],
        rest[KERNEL + 1],
        rest[KERNEL + 2],
        rest[KERNEL + 3],
        up_grad,
        down_grad,
    )


def solution(mesh):
    return jax.shard_map(
        layer,
        mesh=mesh,
        in_specs=(
            P(None, ("dp", "tensor"), "ctx", None),
            P(None, ("dp", "tensor"), None),
            P("dp", None),
            P("dp", None),
            P("dp", None),
            P("dp", None),
            P("dp", None),
            P("dp"),
            P("dp"),
            P("dp"),
            P("dp"),
            P("dp", None, "tensor"),
            P("dp", None, "tensor"),
            P(None, ("dp", "tensor"), "ctx", None),
        ),
        out_specs=(
            P(None, ("dp", "tensor"), "ctx", None),
            P(None, ("dp", "tensor"), "ctx", None),
            P("dp", None),
            P("dp", None),
            P("dp", None),
            P("dp", None),
            P("dp", None),
            P("dp"),
            P("dp"),
            P("dp"),
            P("dp"),
            P("dp", None, "tensor"),
            P("dp", None, "tensor"),
        ),
        check_vma=False,
    )
```
